256 devices in a mesh: req: 32 (over z, y), tp: 8 (over x, core).
Axes of the slice: x: 4, y: 4, z: 8, core: 2. Of those that a mesh axis runs over, the one named last changes fastest.
Arguments:
- hidden: bfloat16 [4096, 8192], P('req'), may hold values from -6 to 6
- input_norm_gain: bfloat16 [8192], replicated, may hold values from 0.25 to 1.75
- wq: bfloat16 [8192, 8192], P('req', 'tp'), as said below
- wk: bfloat16 [8192, 1024], P('req', 'tp'), as said below
- wv: bfloat16 [8192, 1024], P('req', 'tp'), may hold values from -0.0625 to 0.0625
- adapter_down_weight: bfloat16 [64, 48, 8192], P('req', None, 'tp'), may hold values from -0.0625 to 0.0625
- adapter_up_query: bfloat16 [64, 16, 8192], P('req', None, 'tp'), may hold values from -1.5 to 1.5
- adapter_up_key_value: bfloat16 [64, 32, 1024], P('req', None, 'tp'), may hold values from -1.5 to 1.5
- token_request_adapter: int32 [4096], P('req'), may hold values from 0 to 63, as said below
- adapter_storage_slot: int32 [64], replicated, may hold values from 0 to 63, as said below
Outputs:
- context: bfloat16 [4096, 8192], P('req', 'tp')
- keys: bfloat16 [4096, 1024], P('req', 'tp')
- values: bfloat16 [4096, 1024], P('req', 'tp')
The draws below stay inside these ranges and needn't reach their ends.
Inputs may be any that keep to these rules, and one draw needn't show every extreme that they name: `token_request_adapter`: within each aligned block of 128 tokens (the tokens of one index of req), the tokens of one adapter form one contiguous prompt, different prompts of a block use adapters whose slots lie on different holders (slot // 2), and at most 8 tokens of a block use adapters of one holder; in every block some holder gets exactly 8. `adapter_storage_slot`: A permutation of the slots. `wq`: entries of order 8192^-0.5. `wk`: entries of order 8192^-0.5 or more.
All inputs are finite; a program needn't handle non-finite values.
Results may differ from the reference program's by a relative error of at most 0.012.
Values may be sent and summed in bfloat16 or wider, within the bound.
A program may use at most 128 MiB of HBM per device.

```python
import jax
import jax.numpy as jnp
from jax import lax

MODEL_WIDTH = 8192
QUERY_HEADS = 64
KEY_VALUE_HEADS = 8
HEAD_SIZE = 128
ADAPTER_RANK = 16
ADP_DEV = 2
TOKENS_PER_SHARD = 128
ADAPTER_TOTAL = 64
CAP = 8
TOKENS = 4096
N_REQ = 32


def query_matrix(key):
    return jax.random.normal(jax.random.fold_in(key, 11), (MODEL_WIDTH, QUERY_HEADS * HEAD_SIZE), jnp.float32) * MODEL_WIDTH ** (-0.5)


def draw_wq(key, part):
    return query_matrix(key).astype(jnp.bfloat16)


def draw_wk(key, part):
    drawn_projection = jax.random.normal(jax.random.fold_in(key, 12), (MODEL_WIDTH, KEY_VALUE_HEADS * HEAD_SIZE), jnp.float32) * MODEL_WIDTH ** (-0.5)
    return drawn_projection.astype(jnp.bfloat16)


def layout(key):
    slot_of = jax.random.permutation(jax.random.fold_in(key, 31), ADAPTER_TOTAL).astype(jnp.int32)
    adapter_at = jnp.argsort(slot_of).astype(jnp.int32)
    block_keys = jax.random.split(jax.random.fold_in(key, 32), N_REQ)
    order = jax.vmap(lambda one: jax.random.permutation(one, N_REQ))(block_keys).astype(jnp.int32)
    loads = jax.random.randint(jax.random.fold_in(key, 33), (N_REQ, N_REQ), CAP // 2, CAP + 1)
    forced = jax.random.randint(jax.random.fold_in(key, 34), (N_REQ, 1), 0, max(N_REQ // 2, 1))
    loads = jnp.where(jnp.arange(N_REQ)[None, :] == forced, CAP, loads).astype(jnp.int32)
    ends = jnp.cumsum(loads, axis=1)
    steps = jnp.arange(TOKENS_PER_SHARD, dtype=jnp.int32)
    run = jnp.sum((ends[:, None, :] <= steps[None, :, None]).astype(jnp.int32), axis=2).astype(jnp.int32)
    holder = jnp.take_along_axis(order, run, axis=1)
    choose = jax.random.randint(jax.random.fold_in(key, 35), (N_REQ, N_REQ), 0, ADP_DEV).astype(jnp.int32)
    chosen = jnp.take_along_axis(choose, run, axis=1)
    slot = holder * ADP_DEV + chosen
    token_request_adapter = adapter_at[slot].reshape(TOKENS).astype(jnp.int32)
    return (token_request_adapter, slot_of)


def draw_token_request_adapter(key, part):
    return layout(key)[0]


def draw_adapter_storage_slot(key, part):
    return layout(key)[1]


def steps_of(stream_key, dims, shards, smallest, top_value):
    gain = 1.0
    for dim, shards_of in shards:
        heights = jax.random.uniform(jax.random.fold_in(jax.random.fold_in(stream_key, 6), dim), (shards_of,), jnp.float32, smallest / len(shards), top_value / len(shards))
        gain = gain * jnp.repeat(jnp.exp(heights), dims[dim] // shards_of).reshape((-1,) + (1,) * (len(dims) - 1 - dim))
    return gain


def normal_values(rng, shape, scale, limit, cuts=(), held_as=jnp.bfloat16):
    drawn = jax.random.normal(rng, shape, jnp.float32) * scale
    if len(cuts) > 0:
        drawn = steps_of(rng, shape, cuts, -0.22, 0.18) * drawn
    return jnp.clip(drawn, min=-limit, max=limit).astype(held_as)


def setup_inputs(seed: int = 0) -> dict:
    seeds = jax.random.split(jax.random.key(seed), 11)
    return {
        "hidden": normal_values(seeds[0], (TOKENS, MODEL_WIDTH), 1.0, 6.0, ((0, 32),)),
        "input_norm_gain": jnp.clip(1.0 + 0.15 * jax.random.normal(seeds[1], (MODEL_WIDTH,), jnp.float32), 0.25, 1.75).astype(jnp.bfloat16),
        "wq": draw_wq(jax.random.fold_in(seeds[10], 71), 0),
        "wk": draw_wk(jax.random.fold_in(seeds[10], 71), 0),
        "wv": normal_values(seeds[4], (MODEL_WIDTH, KEY_VALUE_HEADS * HEAD_SIZE), MODEL_WIDTH ** -0.5, 0.0625, ((0, 32), (1, 8))),
        "adapter_down_weight": normal_values(seeds[5], (ADAPTER_TOTAL, 3 * ADAPTER_RANK, MODEL_WIDTH), MODEL_WIDTH ** -0.5, 0.0625, ((0, 32), (2, 8))),
        "adapter_up_query": normal_values(seeds[6], (ADAPTER_TOTAL, ADAPTER_RANK, QUERY_HEADS * HEAD_SIZE), ADAPTER_RANK ** -0.5, 1.5, ((0, 32), (2, 8))),
        "adapter_up_key_value": normal_values(seeds[7], (ADAPTER_TOTAL, 2 * ADAPTER_RANK, KEY_VALUE_HEADS * HEAD_SIZE), ADAPTER_RANK ** -0.5, 1.5, ((0, 32), (2, 8))),
        "token_request_adapter": draw_token_request_adapter(jax.random.fold_in(seeds[10], 71), 0),
        "adapter_storage_slot": draw_adapter_storage_slot(jax.random.fold_in(seeds[10], 71), 0),
    }


def apply_up_projection(low_rank_product, selected_entries, table_q, table_kv, adapter_rank_value):
    held_adapters = selected_entries.shape[-1]

    def widen(piece):
        return (selected_entries[..., :, None] * piece[..., None, :]).reshape(piece.shape[:-1] + (held_adapters * adapter_rank_value,))
    part_q = jnp.dot(widen(low_rank_product[..., :adapter_rank_value]), table_q.reshape(held_adapters * adapter_rank_value, -1), preferred_element_type=jnp.float32)
    part_k = jnp.dot(widen(low_rank_product[..., adapter_rank_value:2 * adapter_rank_value]), table_kv[:, :adapter_rank_value].reshape(held_adapters * adapter_rank_value, -1), preferred_element_type=jnp.float32)
    part_v = jnp.dot(widen(low_rank_product[..., 2 * adapter_rank_value:]), table_kv[:, adapter_rank_value:].reshape(held_adapters * adapter_rank_value, -1), preferred_element_type=jnp.float32)
    return jnp.concatenate([part_q, part_k, part_v], axis=-1).astype(jnp.bfloat16)

def rotate(field, position, head_dim):
    count = field.shape[0]
    heads = field.shape[1] // head_dim
    half = head_dim // 2
    freq = 10000.0 ** (-(jnp.arange(half, dtype=jnp.float32) * 2.0 / head_dim))
    angle = position.astype(jnp.float32)[:, None] * freq[None, :]
    cosine = jnp.cos(angle)[:, None, :]
    sine = jnp.sin(angle)[:, None, :]
    shaped = field.reshape(count, heads, head_dim)
    first = shaped[..., :half]
    second = shaped[..., half:]
    turned = jnp.concatenate([first * cosine - second * sine, second * cosine + first * sine], axis=-1)
    return turned.reshape(count, heads * head_dim)

def reference(hidden, input_norm_gain, wq, wk, wv, adapter_down_weight, adapter_up_query, adapter_up_key_value, token_request_adapter, adapter_storage_slot):
    wide = hidden.astype(jnp.float32)
    scale = lax.rsqrt(lax.optimization_barrier(jnp.mean(wide * wide, axis=-1, keepdims=True)) + 1e-05)
    normed = (wide * scale * input_norm_gain.astype(jnp.float32)[None, :]).astype(jnp.bfloat16)
    base_q = jnp.dot(normed, wq, preferred_element_type=jnp.float32)
    base_k = jnp.dot(normed, wk, preferred_element_type=jnp.float32)
    base_v = jnp.dot(normed, wv, preferred_element_type=jnp.float32)
    slot = adapter_storage_slot[token_request_adapter]
    adapter_table = adapter_down_weight.reshape(ADAPTER_TOTAL * 3 * ADAPTER_RANK, MODEL_WIDTH)
    low_all = jnp.dot(normed, adapter_table.T, preferred_element_type=jnp.float32).reshape(TOKENS, ADAPTER_TOTAL, 3 * ADAPTER_RANK)
    selected_entries = (slot[:, None] == jnp.arange(ADAPTER_TOTAL, dtype=jnp.int32)[None, :]).astype(jnp.float32)
    low_rank_product = lax.optimization_barrier(jnp.sum(low_all * selected_entries[:, :, None], axis=1)).astype(jnp.bfloat16)
    adapter_delta = apply_up_projection(low_rank_product, selected_entries.astype(jnp.bfloat16), adapter_up_query, adapter_up_key_value, ADAPTER_RANK).astype(jnp.float32)
    q_width = QUERY_HEADS * HEAD_SIZE
    key_value_width = KEY_VALUE_HEADS * HEAD_SIZE
    query = base_q + 0.5 * adapter_delta[:, :q_width]
    key = base_k + 0.5 * adapter_delta[:, q_width:q_width + key_value_width]
    value = base_v + 0.5 * adapter_delta[:, q_width + key_value_width:]
    blocked = token_request_adapter.reshape(N_REQ, TOKENS_PER_SHARD)
    steps = jnp.arange(TOKENS_PER_SHARD, dtype=jnp.int32)
    same = blocked[:, :, None] == blocked[:, None, :]
    earlier = same & (steps[None, None, :] < steps[None, :, None])
    position = lax.optimization_barrier(jnp.sum(earlier.astype(jnp.int32), axis=2)).astype(jnp.int32).reshape(TOKENS)
    visible = same & (steps[None, None, :] <= steps[None, :, None])
    query_rotated = rotate(query, position, HEAD_SIZE).astype(jnp.bfloat16)
    keys = rotate(key, position, HEAD_SIZE).astype(jnp.bfloat16)
    values = value.astype(jnp.bfloat16)
    token_group = QUERY_HEADS // KEY_VALUE_HEADS
    query_block_list = query_rotated.reshape(N_REQ, TOKENS_PER_SHARD, KEY_VALUE_HEADS, token_group, HEAD_SIZE)
    key_block_list = keys.reshape(N_REQ, TOKENS_PER_SHARD, KEY_VALUE_HEADS, HEAD_SIZE)
    value_block_list = values.reshape(N_REQ, TOKENS_PER_SHARD, KEY_VALUE_HEADS, HEAD_SIZE)

    def one_block(items):
        q_here, k_here, v_here, seen = items
        scores = jnp.einsum('tkgd,skd->kgts', q_here.astype(jnp.float32), k_here.astype(jnp.float32)) / jnp.sqrt(jnp.float32(HEAD_SIZE))
        scores = jnp.where(seen[None, None, :, :], scores, jnp.float32(-1e+30))
        top = lax.optimization_barrier(jnp.max(scores, axis=-1, keepdims=True))
        raised = jnp.exp(scores - top)
        weights = (raised / lax.optimization_barrier(jnp.sum(raised, axis=-1, keepdims=True))).astype(jnp.bfloat16)
        mixed = jnp.einsum('kgts,skd->tkgd', weights.astype(jnp.float32), v_here.astype(jnp.float32))
        return mixed.astype(jnp.bfloat16)
    context = lax.map(one_block, (query_block_list, key_block_list, value_block_list, visible))
    return (context.reshape(TOKENS, QUERY_HEADS * HEAD_SIZE), keys, values)
```

```python
import jax
import jax.numpy as jnp
from jax import lax
from jax.sharding import PartitionSpec as P

HEAD_SIZE = 128
NY = 4
NZ = 8
ROWS = 32


def rotate(field, position, head_dim):
    count = field.shape[0]
    heads = field.shape[1] // head_dim
    half = head_dim // 2
    freq = 10000.0 ** (-(jnp.arange(half, dtype=jnp.float32) * 2.0 / head_dim))
    angle = position.astype(jnp.float32)[:, None] * freq[None, :]
    cosine = jnp.cos(angle)[:, None, :]
    sine = jnp.sin(angle)[:, None, :]
    shaped = field.reshape(count, heads, head_dim)
    first = shaped[..., :half]
    second = shaped[..., half:]
    turned = jnp.concatenate(
        [first * cosine - second * sine, second * cosine + first * sine], axis=-1
    )
    return turned.reshape(count, heads * head_dim)


def per_device(
    hidden,
    input_norm_gain,
    wq,
    wk,
    wv,
    adapter_down_weight,
    adapter_up_query,
    adapter_up_key_value,
    token_request_adapter,
    adapter_storage_slot,
):
    groups_y = [[z * NY + y for y in range(NY)] for z in range(NZ)]
    groups_z = [[z * NY + y for z in range(NZ)] for y in range(NY)]
    tokens, width = hidden.shape
    my_req = lax.axis_index("req")
    my_z = my_req // NY
    my_tp = lax.axis_index("tp")
    part = width // NZ
    wide = hidden.astype(jnp.float32)
    scale = lax.rsqrt(jnp.mean(wide * wide, axis=-1, keepdims=True) + 1e-05)
    normed = (wide * scale * input_norm_gain.astype(jnp.float32)[None, :]).astype(jnp.bfloat16)

    count = adapter_storage_slot.shape[0]
    match = token_request_adapter[:, None] == jnp.arange(count, dtype=jnp.int32)[None, :]
    slot = jnp.sum(jnp.where(match, adapter_storage_slot[None, :], 0), axis=1)
    plane = slot // 8
    steps = jnp.arange(tokens, dtype=jnp.int32)
    before = steps[None, :] < steps[:, None]
    same = (slot[:, None] // 2) == (slot[None, :] // 2)
    position = jnp.sum((same & before).astype(jnp.int32), axis=1)
    visible = same & (steps[None, :] <= steps[:, None])
    rank = jnp.sum(((plane[:, None] == plane[None, :]) & before).astype(jnp.int32), axis=1)

    w_q = lax.all_gather(wq, "req", axis=0, tiled=True, axis_index_groups=groups_y)
    w_kv = lax.all_gather(
        jnp.concatenate([wk, wv], axis=1), "req", axis=0, tiled=True, axis_index_groups=groups_y
    )
    down = lax.all_gather(
        adapter_down_weight, "req", axis=0, tiled=True, axis_index_groups=groups_y
    )
    up_q = lax.all_gather(adapter_up_query, "req", axis=0, tiled=True, axis_index_groups=groups_y)
    up_kv = lax.all_gather(
        adapter_up_key_value, "req", axis=0, tiled=True, axis_index_groups=groups_y
    )

    mine = lax.dynamic_slice_in_dim(normed, my_tp * 16, 16, 0).reshape(16, NZ, part)
    got = lax.all_to_all(
        mine, "req", split_axis=1, concat_axis=1, axis_index_groups=groups_z, tiled=True
    )
    acts = lax.all_gather(got, "tp", axis=0, tiled=True)
    acts = jnp.swapaxes(acts, 0, 1).reshape(NZ * tokens, part)

    code = lax.all_gather(slot * 256 + rank, "req", axis=0, tiled=True, axis_index_groups=groups_z)
    all_slot = code // 256
    all_rank = code % 256

    target = plane * ROWS + rank
    place = (target[None, :] == jnp.arange(NZ * ROWS, dtype=jnp.int32)[:, None]).astype(
        jnp.bfloat16
    )
    feature_part = lax.dynamic_slice_in_dim(normed, my_tp * part, part, 1)
    rows = (
        jnp.dot(place, feature_part, preferred_element_type=jnp.float32)
        .astype(jnp.bfloat16)
        .reshape(NZ, ROWS, part)
    )
    rows = lax.all_to_all(
        rows, "req", split_axis=0, concat_axis=0, axis_index_groups=groups_z, tiled=True
    ).reshape(NZ * ROWS, part)
    low_all = lax.dot_general(
        rows, down.reshape(8 * 48, part), (((1,), (1,)), ((), ())),
        preferred_element_type=jnp.float32,
    )
    low_all = lax.psum(low_all, "tp")

    block = jnp.arange(NZ * tokens, dtype=jnp.int32) // tokens
    all_target = jnp.where(all_slot // 8 == my_z, block * ROWS + all_rank, -1)
    spread = (all_target[:, None] == jnp.arange(NZ * ROWS, dtype=jnp.int32)[None, :]).astype(
        jnp.bfloat16
    )
    low_tok = jnp.dot(
        spread, low_all.astype(jnp.bfloat16), preferred_element_type=jnp.float32
    ).reshape(NZ * tokens, 8, 48)
    pick = (all_slot % 8)[:, None] == jnp.arange(8, dtype=jnp.int32)[None, :]
    low_tok = jnp.where(pick[:, :, None], low_tok, 0.0).astype(jnp.bfloat16)

    def up(lo, table):
        return jnp.dot(
            low_tok[:, :, lo : lo + 16].reshape(NZ * tokens, 128),
            table.reshape(128, -1),
            preferred_element_type=jnp.float32,
        ).astype(jnp.bfloat16)

    delta = jnp.concatenate(
        [up(0, up_q), up(16, up_kv[:, :16]), up(32, up_kv[:, 16:])], axis=1
    ).astype(jnp.float32)
    base = jnp.concatenate(
        [
            jnp.dot(acts, w_q, preferred_element_type=jnp.float32),
            jnp.dot(acts, w_kv, preferred_element_type=jnp.float32),
        ],
        axis=1,
    )
    part_out = (base + 0.5 * delta).astype(jnp.bfloat16)
    full = lax.psum_scatter(
        part_out, "req", scatter_dimension=0, axis_index_groups=groups_z, tiled=True
    ).astype(jnp.float32)

    query = full[:, :1024]
    key = full[:, 1024:1152]
    value = full[:, 1152:]
    head_dim = HEAD_SIZE
    q_rot = rotate(query, position, head_dim).astype(jnp.bfloat16)
    keys = rotate(key, position, head_dim).astype(jnp.bfloat16)
    values = value.astype(jnp.bfloat16)
    q_heads = q_rot.reshape(tokens, 8, head_dim)
    scores = jnp.einsum(
        "tgd,sd->gts", q_heads, keys, preferred_element_type=jnp.float32
    ) / jnp.sqrt(jnp.float32(head_dim))
    scores = jnp.where(visible[None], scores, jnp.float32(-1e30))
    top = jnp.max(scores, axis=-1, keepdims=True)
    raised = jnp.exp(scores - top)
    weights = (raised / jnp.sum(raised, axis=-1, keepdims=True)).astype(jnp.bfloat16)
    context = jnp.einsum("gts,sd->tgd", weights, values, preferred_element_type=jnp.float32)
    return (context.astype(jnp.bfloat16).reshape(tokens, 1024), keys, values)


def solution(mesh):
    in_specs = (
        P("req", None),
        P(),
        P("req", "tp"),
        P("req", "tp"),
        P("req", "tp"),
        P("req", None, "tp"),
        P("req", None, "tp"),
        P("req", None, "tp"),
        P("req"),
        P(),
    )
    out_specs = (P("req", "tp"), P("req", "tp"), P("req", "tp"))
    return jax.shard_map(
        per_device, mesh=mesh, in_specs=in_specs, out_specs=out_specs, check_vma=False
    )
```

```python
import functools

import jax
import jax.numpy as jnp
import numpy as np
from jax import lax
from jax.experimental import pallas as pl
from jax.experimental.pallas import tpu as pltpu
from jax.sharding import PartitionSpec as P

MESH = pl.DeviceIdType.MESH
HEAD = 128
NY = 4
NZ = 8
NT = 8
TOK = 128
WIDTH = 8192
PART = 1024
CW = 256
ROWS = 32
CHUNKS = 5
BF = jnp.bfloat16
F32 = jnp.float32
ORDER = (0, 1, 7, 2, 6, 3, 5, 4)
POS = tuple(ORDER.index(r) for r in range(NZ))
GROUPS = ((1, 2), (3, 2), (5, 3))
AHEAD = 5


def longest(c, way):
    return 4 if way == (1 if c % 2 == 0 else 0) else 3


def body(
    hid, gain, tra, sas, rope, wq, wk, wv, dn, uq, ukv,
    ctx, kout, vout,
    hidv, scale, act, asend, meta_s, meta_r, rsend, rrecv,
    wqb, wkvb, db, uqb, ukvb,
    place, low_s, low_r, low_l, part, sendb, recvb, cosb, sinb, visb,
    loc_sem, y_ss, y_rs, a_ss, a_rs, m_ss, m_rs, r_ss, r_rs,
    x_ss, x_rs, p_ss, p_rs, l_ss, l_rs, z_ss, z_rs,
):
    req = lax.axis_index("req")
    tp = lax.axis_index("tp")
    z = req // NY
    y = req % NY
    core = tp % 2
    partner = tp + 1 - 2 * core

    def zdev(q):
        return {"req": lax.rem(z + q + NZ, NZ) * NY + y, "tp": tp}

    def ydev(q):
        return {"req": z * NY + lax.rem(y + q + NY, NY), "tp": tp}

    def tdev(q):
        return {"req": req, "tp": lax.rem(tp + q + NT, NT)}

    partner_dev = {"req": req, "tp": partner}

    def remote(src, dst, ss, rs, dev):
        return pltpu.make_async_remote_copy(
            src_ref=src, dst_ref=dst, send_sem=ss, recv_sem=rs, device_id=dev, device_id_type=MESH
        )

    pending = []

    def go(copy):
        copy.start()
        pending.append(copy)

    def rows2(buf, yb):
        return buf.at[pl.ds(2 * yb, 2)]

    def rows2h(buf, yb, h):
        return buf.at[pl.ds(2 * yb + h, 1)]

    def cols(buf, yb, lo, wide):
        return buf.at[pl.ds(pl.multiple_of(yb * 256, 256), 256), pl.ds(lo, wide)]

    def colsh(buf, yb, h, lo, wide):
        return buf.at[pl.ds(pl.multiple_of(yb * 256 + h * 128, 128), 128), pl.ds(lo, wide)]

    items = [
        (dn, functools.partial(rows2, db), functools.partial(rows2h, db)),
        (uq, functools.partial(rows2, uqb), functools.partial(rows2h, uqb)),
        (ukv, functools.partial(rows2, ukvb), functools.partial(rows2h, ukvb)),
        (wk, lambda b: cols(wkvb, b, 0, 128), lambda b, h: colsh(wkvb, b, h, 0, 128)),
        (wv, lambda b: cols(wkvb, b, 128, 128), lambda b, h: colsh(wkvb, b, h, 128, 128)),
    ]
    for j in range(4):
        items.append((
            wq.at[:, pl.ds(CW * j, CW)],
            lambda b, j=j: cols(wqb, b, CW * j, CW),
            lambda b, h, j=j: colsh(wqb, b, h, CW * j, CW),
        ))
    yl = lax.rem(y + NY - 1, NY)
    yr = lax.rem(y + 1, NY)

    def y_first(i, way):
        src, region, _ = items[i]
        return remote(
            src, region(y), y_ss.at[i, way], y_rs.at[i, way], ydev(1 if way == 0 else -1)
        )

    def y_second(i, way):
        _, _, half = items[i]
        ref = half(yl if way == 0 else yr, way)
        return remote(
            ref, ref, y_ss.at[i, 2 + way], y_rs.at[i, 2 + way], ydev(1 if way == 0 else -1)
        )

    def y_start(i):
        if i < len(items):
            go(y_first(i, 0))
            go(y_first(i, 1))

    def y_pump(i):
        for way in range(2):
            y_first(i, way).wait_recv()
            go(y_second(i, way))
        y_start(i + AHEAD)

    def y_wait(i):
        y_second(i, 0).wait_recv()
        y_second(i, 1).wait_recv()

    hid_copy = pltpu.make_async_copy(hid, hidv, loc_sem.at[0])
    hid_copy.start()
    own = []
    for i in range(len(items)):
        src, region, _ = items[i]
        copy = pltpu.make_async_copy(src, region(y), loc_sem.at[1 + i])
        copy.start()
        own.append(copy)

    barrier = pltpu.get_barrier_semaphore()
    for q in range(1, NZ):
        pl.semaphore_signal(barrier, inc=1, device_id=zdev(q), device_id_type=MESH)
    for q in range(1, NT):
        pl.semaphore_signal(barrier, inc=1, device_id=tdev(q), device_id_type=MESH)
    for q in (1, -1):
        pl.semaphore_signal(barrier, inc=1, device_id=ydev(q), device_id_type=MESH)

    lane = lax.broadcasted_iota(jnp.int32, (TOK, TOK), 1)
    sub = lax.broadcasted_iota(jnp.int32, (TOK, TOK), 0)
    tra_c = jnp.transpose(jnp.broadcast_to(tra[...].astype(F32), (TOK, TOK))).astype(jnp.int32)
    sas_r = jnp.broadcast_to(sas[...].astype(F32), (TOK, TOK))
    slot_c = jnp.sum(jnp.where(tra_c == lane, sas_r, 0.0), axis=1, keepdims=True)
    slot_cm = jnp.broadcast_to(slot_c, (TOK, TOK))
    slot_rm = jnp.transpose(slot_cm).astype(jnp.int32)
    slot_cm = slot_cm.astype(jnp.int32)
    same = (slot_cm >> 1) == (slot_rm >> 1)
    pos_c = jnp.sum(jnp.where(same & (lane < sub), 1.0, 0.0), axis=1, keepdims=True)
    visb[...] = jnp.where(same & (lane <= sub), 1.0, 0.0)
    flat = (slot_cm >> 3) == (slot_rm >> 3)
    rank_r = jnp.sum(jnp.where(flat & (sub < lane), 1.0, 0.0), axis=0, keepdims=True)
    slot_r = slot_rm[0:1, :]
    code_r = slot_r.astype(F32) * 32.0 + rank_r
    meta_s[...] = jnp.broadcast_to(code_r, (8, TOK))
    meta_r[:, 0:TOK] = jnp.broadcast_to(code_r, (8, TOK))
    pos_m = jnp.broadcast_to(pos_c, (TOK, TOK))
    cos = jnp.zeros((TOK, TOK), F32)
    sin = jnp.zeros((TOK, TOK), F32)
    for p in range(8):
        here = pos_m == float(p)
        cos = jnp.where(here, rope[p : p + 1, :], cos)
        sin = jnp.where(here, rope[8 + p : 9 + p, :], sin)
    cosb[...] = cos
    sinb[...] = sin

    hid_copy.wait()

    def stat(i, carry):
        rows = pl.ds(pl.multiple_of(i * 16, 16), 16)
        total = jnp.zeros((16, 128), F32)
        for k in range(8):
            x = hidv[rows, pl.ds(k * 1024, 1024)].astype(F32)
            x = x * x
            for m in range(8):
                total = total + x[:, 128 * m : 128 * m + 128]
        mean = jnp.sum(total, axis=1, keepdims=True) * (1.0 / WIDTH)
        scale[rows, :] = jnp.broadcast_to(lax.rsqrt(mean + 1e-05), (16, 128))
        return carry

    lax.fori_loop(0, 8, stat, 0)

    pl.semaphore_wait(barrier, 7 + 7 + 2)
    for i in range(AHEAD):
        y_start(i)

    my_rows = pl.ds(pl.multiple_of(tp * 16, 16), 16)
    s16 = scale[my_rows, :][:, 0:1]
    for j in range(NZ):
        c = pl.ds(j * PART, PART)
        asend[j] = (
            hidv[my_rows, c].astype(F32) * s16 * gain[0:1, c].astype(F32)
        ).astype(BF)

    def a_copy(q):
        k = POS[(-q) % NZ]
        return remote(
            asend.at[lax.rem(z + q, NZ)], act.at[k, my_rows, :],
            a_ss.at[k], a_rs.at[k], zdev(q),
        )

    def m_copy(q):
        k = POS[(-q) % NZ]
        return remote(
            meta_s, meta_r.at[:, pl.ds(k * TOK, TOK)], m_ss.at[k], m_rs.at[k], zdev(q)
        )

    for q in ORDER[1:]:
        go(a_copy(q))
    for q in ORDER[1:]:
        go(m_copy(q))

    def normed(start):
        c = pl.ds(pl.multiple_of(start, PART), PART)
        return (hidv[:, c].astype(F32) * scale[:, 0:1] * gain[0:1, c].astype(F32)).astype(BF)

    target = (slot_rm >> 3) * ROWS + jnp.broadcast_to(rank_r, (TOK, TOK)).astype(jnp.int32)
    sub2 = lax.broadcasted_iota(jnp.int32, (NZ * ROWS, TOK), 0)
    put = jnp.where(
        sub2 == jnp.concatenate([target, target], axis=0), 1.0, 0.0
    ).astype(BF)
    rsend[...] = jnp.dot(put, normed(tp * PART), preferred_element_type=F32).astype(BF)

    def r_block(b):
        return pl.ds(pl.multiple_of(b * ROWS, ROWS), ROWS)

    def r_copy(q):
        k = POS[(-q) % NZ]
        return remote(
            rsend.at[r_block(lax.rem(z + q, NZ)), :], rrecv.at[pl.ds(k * ROWS, ROWS), :],
            r_ss.at[k], r_rs.at[k], zdev(q),
        )

    for q in ORDER[1:]:
        go(r_copy(q))
    rrecv[0:ROWS, :] = rsend[r_block(z), :]
    act[0] = normed(z * PART)

    def t_rows(q):
        return pl.ds(pl.multiple_of(lax.rem(tp + q + NT, NT) * 16, 16), 16)

    def x_region(g, q, half=None):
        lo, n = GROUPS[g]
        if half is None:
            return act.at[pl.ds(lo, n), t_rows(q), :]
        return act.at[pl.ds(lo, n), t_rows(q), pl.ds(512 * half, 512)]

    def x_first(g, way):
        ref = x_region(g, 0)
        return remote(ref, ref, x_ss.at[g, way], x_rs.at[g, way], tdev(2 if way == 0 else -2))

    def x_second(g, way):
        ref = x_region(g, -2 if way == 0 else 2, way)
        return remote(
            ref, ref, x_ss.at[g, 2 + way], x_rs.at[g, 2 + way], tdev(2 if way == 0 else -2)
        )

    def p_copy(g, k):
        ref = x_region(g, (0, -2, 2, 4)[k])
        return remote(ref, ref, p_ss.at[g, k], p_rs.at[g, k], partner_dev)

    def x_send(g):
        lo, n = GROUPS[g]
        for k in range(lo, lo + n):
            a_copy((-ORDER[k]) % NZ).wait_recv()
        go(x_first(g, 0))
        go(x_first(g, 1))
        go(p_copy(g, 0))

    def x_forward(g):
        for way in range(2):
            x_first(g, way).wait_recv()
            go(x_second(g, way))
            go(p_copy(g, 1 + way))

    def x_last(g):
        x_second(g, 0).wait_recv()
        x_second(g, 1).wait_recv()
        go(p_copy(g, 3))

    x_send(0)
    x_send(1)
    y_pump(0)
    x_send(2)
    x_forward(0)
    y_pump(1)
    y_pump(2)
    x_forward(1)
    x_last(0)
    y_pump(3)
    x_forward(2)
    x_last(1)
    y_pump(4)
    x_last(2)
    for g in range(3):
        for k in range(4):
            p_copy(g, k).wait_recv()

    for copy in own:
        copy.wait()

    def base(c):
        def tile(i, carry):
            a = act[pl.ds(2 * i, 2)].reshape(2 * TOK, PART)
            w = wkvb[...] if c == 0 else wqb[:, CW * (c - 1) : CW * c]
            part[c, pl.ds(2 * i, 2)] = jnp.dot(a, w, preferred_element_type=F32).reshape(
                2, TOK, CW
            )
            return carry

        lax.fori_loop(0, NZ // 2, tile, 0)

    y_wait(3)
    y_wait(4)
    base(0)
    y_pump(5)

    for q in ORDER[1:]:
        m_copy(q).wait_recv()
    lane2 = lax.broadcasted_iota(jnp.int32, (TOK, NZ * ROWS), 1)
    a8_row = jnp.zeros((8, NZ * ROWS), F32)
    for k in range(NZ):
        code = meta_r[0:8, k * TOK : (k + 1) * TOK]
        code_c = jnp.transpose(jnp.broadcast_to(code[0:1, :], (TOK, TOK))).astype(jnp.int32)
        slot_k = code_c[:, 0:1] >> 5
        rank_k = code_c[:, 0:1] & 31
        want = jnp.where((slot_k >> 3) == z, k * ROWS + rank_k, -1)
        hot = jnp.where(lane2 == want, 1.0, 0.0).astype(BF)
        place[k] = hot
        a8 = ((code.astype(jnp.int32) >> 5) & 7).astype(F32).astype(BF)
        a8_row = a8_row + jnp.dot(a8, hot, preferred_element_type=F32)

    y_wait(0)
    for q in ORDER[1:]:
        r_copy(q).wait_recv()
    low_all = lax.dot_general(
        db[...].reshape(8 * 48, PART), rrecv[...], (((1,), (1,)), ((), ())),
        preferred_element_type=F32,
    )
    low_mine = jnp.zeros((48, NZ * ROWS), F32)
    for a in range(8):
        low_mine = low_mine + jnp.where(
            a8_row[0:1, :] == float(a), low_all[48 * a : 48 * a + 48, :], 0.0
        )
    low_s[...] = low_mine.astype(BF)

    def l_copy(q):
        return remote(low_s, low_r.at[q], l_ss.at[q], l_rs.at[q], tdev(q))

    for q in range(1, NT):
        go(l_copy(q))
    y_wait(5)
    base(1)
    y_pump(6)
    for q in range(1, NT):
        l_copy(q).wait_recv()
    low_sum = low_mine
    for q in range(1, NT):
        low_sum = low_sum + low_r[q].astype(F32)
    low_sum = low_sum.astype(BF)
    wide = jnp.concatenate(
        [low_sum[0:16]] * 8 + [low_sum[16:32]] * 8 + [low_sum[32:48]] * 8, axis=0
    )
    lane3 = lax.broadcasted_iota(jnp.int32, (TOK, 384), 1)
    for k in range(NZ):
        code = meta_r[0:1, k * TOK : (k + 1) * TOK]
        code_c = jnp.transpose(jnp.broadcast_to(code, (TOK, TOK))).astype(jnp.int32)
        a8_k = (code_c[:, 0:1] >> 5) & 7
        got = lax.dot_general(
            place[k], wide, (((1,), (1,)), ((), ())), preferred_element_type=F32
        )
        low_l[k] = jnp.where(((lane3 >> 4) & 7) == a8_k, got, 0.0).astype(BF)

    y_wait(1)
    y_wait(2)

    def z_copy(c, way, h):
        k = POS[h if way == 0 else NZ - h]
        return remote(
            sendb.at[c, k], recvb.at[c, way, h - 1], z_ss.at[c, way, h - 1],
            z_rs.at[c, way, h - 1], zdev(1 if way == 0 else -1),
        )

    def correct(c):
        def tile(i, carry):
            ll = low_l[pl.ds(2 * i, 2)].reshape(2 * TOK, 384)
            if c == 0:
                u_k = ukvb[:, 0:16, :].reshape(128, 128)
                u_v = ukvb[:, 16:32, :].reshape(128, 128)
                d = jnp.concatenate(
                    [
                        jnp.dot(ll[:, 128:256], u_k, preferred_element_type=F32),
                        jnp.dot(ll[:, 256:384], u_v, preferred_element_type=F32),
                    ],
                    axis=1,
                )
            else:
                u_q = uqb[:, :, CW * (c - 1) : CW * c].reshape(128, CW)
                d = jnp.dot(ll[:, 0:128], u_q, preferred_element_type=F32)
            d = 0.5 * d.astype(BF).astype(F32)
            part[c, pl.ds(2 * i, 2)] += d.reshape(2, TOK, CW)
            return carry

        lax.fori_loop(0, NZ // 2, tile, 0)

    for c in range(CHUNKS):
        if c >= 2:
            y_wait(4 + c)
            base(c)
            if c < 4:
                y_pump(5 + c)
        correct(c)
        way = 0 if longest(c, 0) == 4 else 1
        k = POS[4]
        sendb[c, k] = part[c, k].astype(BF)
        go(z_copy(c, way, 4))
    for h in (3, 2, 1):
        for c in range(CHUNKS):
            for way in range(2):
                k = POS[h if way == 0 else NZ - h]
                total = part[c, k]
                if h + 1 <= longest(c, way):
                    z_copy(c, way, h + 1).wait_recv()
                    total = total + recvb[c, way, h].astype(F32)
                sendb[c, k] = total.astype(BF)
                go(z_copy(c, way, h))

    def final(c):
        z_copy(c, 0, 1).wait_recv()
        z_copy(c, 1, 1).wait_recv()
        return part[c, 0] + recvb[c, 0, 0].astype(F32) + recvb[c, 1, 0].astype(F32)

    cos = cosb[...]
    sin = sinb[...]

    def turn(u):
        return u * cos + pltpu.roll(u, HEAD // 2, 1) * sin

    kv = final(0)
    keys = turn(kv[:, 0:HEAD]).astype(BF)
    values = kv[:, HEAD:].astype(BF)
    kout[...] = keys
    vout[...] = values
    seen = visb[...] > 0.5
    root = float(np.float32(1.0) / np.sqrt(np.float32(HEAD)))
    for c in range(1, CHUNKS):
        both = final(c)
        for i in range(2):
            query = turn(both[:, HEAD * i : HEAD * (i + 1)]).astype(BF)
            scores = lax.dot_general(
                query, keys, (((1,), (1,)), ((), ())), preferred_element_type=F32
            ) * root
            scores = jnp.where(seen, scores, -1e30)
            raised = jnp.exp(scores - jnp.max(scores, axis=1, keepdims=True))
            weights = (raised / jnp.sum(raised, axis=1, keepdims=True)).astype(BF)
            lo = CW * (c - 1) + HEAD * i
            ctx[:, lo : lo + HEAD] = jnp.dot(
                weights, values, preferred_element_type=F32
            ).astype(BF)

    for copy in pending:
        copy.wait_send()


def rope_table():
    half = HEAD // 2
    freq = np.float32(10000.0) ** (-(np.arange(half, dtype=np.float32) * np.float32(2.0) / HEAD))
    angle = np.arange(8, dtype=np.float32)[:, None] * freq[None, :].astype(np.float32)
    cos = np.cos(angle).astype(np.float32)
    sin = np.sin(angle).astype(np.float32)
    return np.concatenate(
        [np.concatenate([cos, cos], axis=1), np.concatenate([-sin, sin], axis=1)], axis=0
    )


def per_device(hidden, gain, wq, wk, wv, down, up_q, up_kv, adapter, storage):
    any_spec = pl.BlockSpec(memory_space=pl.ANY)
    vmem = pl.BlockSpec(memory_space=pltpu.VMEM)
    dma = pltpu.SemaphoreType.DMA
    count = storage.shape[0]
    call = pl.pallas_call(
        body,
        out_shape=(
            jax.ShapeDtypeStruct((TOK, PART), BF),
            jax.ShapeDtypeStruct((TOK, HEAD), BF),
            jax.ShapeDtypeStruct((TOK, HEAD), BF),
        ),
        in_specs=[any_spec, vmem, vmem, vmem, vmem] + [any_spec] * 6,
        out_specs=(vmem, vmem, vmem),
        scratch_shapes=[
            pltpu.VMEM((TOK, WIDTH), BF),
            pltpu.VMEM((TOK, 128), F32),
            pltpu.VMEM((NZ, TOK, PART), BF),
            pltpu.VMEM((NZ, 16, PART), BF),
            pltpu.VMEM((8, TOK), F32),
            pltpu.VMEM((8, NZ * TOK), F32),
            pltpu.VMEM((NZ * ROWS, PART), BF),
            pltpu.VMEM((NZ * ROWS, PART), BF),
            pltpu.VMEM((PART, PART), BF),
            pltpu.VMEM((PART, CW), BF),
            pltpu.VMEM((8, 48, PART), BF),
            pltpu.VMEM((8, 16, PART), BF),
            pltpu.VMEM((8, 32, HEAD), BF),
            pltpu.VMEM((NZ, TOK, NZ * ROWS), BF),
            pltpu.VMEM((48, NZ * ROWS), BF),
            pltpu.VMEM((NT, 48, NZ * ROWS), BF),
            pltpu.VMEM((NZ, TOK, 384), BF),
            pltpu.VMEM((CHUNKS, NZ, TOK, CW), F32),
            pltpu.VMEM((CHUNKS, NZ, TOK, CW), BF),
            pltpu.VMEM((CHUNKS, 2, 4, TOK, CW), BF),
            pltpu.VMEM((TOK, TOK), F32),
            pltpu.VMEM((TOK, TOK), F32),
            pltpu.VMEM((TOK, TOK), F32),
            dma((10,)),
            dma((9, 4)), dma((9, 4)),
            dma((NZ,)), dma((NZ,)),
            dma((NZ,)), dma((NZ,)),
            dma((NZ,)), dma((NZ,)),
            dma((3, 4)), dma((3, 4)),
            dma((3, 4)), dma((3, 4)),
            dma((NT,)), dma((NT,)),
            dma((CHUNKS, 2, 4)), dma((CHUNKS, 2, 4)),
        ],
        compiler_params=pltpu.CompilerParams(
            collective_id=0, has_side_effects=True, vmem_limit_bytes=60 * 1024 * 1024
        ),
    )
    return call(
        hidden,
        gain.reshape(1, WIDTH),
        adapter.reshape(1, TOK),
        jnp.pad(storage.reshape(1, count), ((0, 0), (0, TOK - count))),
        jnp.asarray(rope_table()),
        wq, wk, wv, down, up_q, up_kv,
    )


def solution(mesh):
    in_specs = (
        P("req", None),
        P(),
        P("req", "tp"),
        P("req", "tp"),
        P("req", "tp"),
        P("req", None, "tp"),
        P("req", None, "tp"),
        P("req", None, "tp"),
        P("req"),
        P(),
    )
    out_specs = (P("req", "tp"), P("req", "tp"), P("req", "tp"))
    return jax.shard_map(
        per_device, mesh=mesh, in_specs=in_specs, out_specs=out_specs, check_vma=False
    )
```

```python
import functools

import jax
import jax.numpy as jnp
import numpy as np
from jax import lax
from jax.experimental import pallas as pl
from jax.experimental.pallas import tpu as pltpu
from jax.sharding import PartitionSpec as P

MESH = pl.DeviceIdType.MESH
HEAD = 128
NY = 4
NZ = 8
NT = 8
TOK = 128
WIDTH = 8192
PART = 1024
CW = 256
ROWS = 32
CHUNKS = 5
BF = jnp.bfloat16
F32 = jnp.float32
ORDER = (0, 1, 7, 2, 6, 3, 5, 4)
POS = tuple(ORDER.index(r) for r in range(NZ))
GROUPS = ((1, 2), (3, 2), (5, 3))
AHEAD = 3


def longest(c, way):
    return 4 if way == (1 if c % 2 == 0 else 0) else 3


def body(
    hid, gain, tra, sas, rope, wq, wk, wv, dn, uq, ukv,
    ctx, kout, vout,
    hidv, hid16, gainf, scale, act, asend, meta_s, meta_r, rsend, rrecv,
    wqb, wkvb, db, uqb, ukvb,
    place, a8_of, low_s, low_r, low_l, part, sendb, recvb, cosb, sinb, visb,
    loc_sem, y_ss, y_rs, a_ss, a_rs, m_ss, m_rs, r_ss, r_rs,
    x_ss, x_rs, p_ss, p_rs, l_ss, l_rs, z_ss, z_rs,
):
    req = lax.axis_index("req")
    tp = lax.axis_index("tp")
    z = req // NY
    y = req % NY
    core = tp % 2
    partner = tp + 1 - 2 * core

    def zdev(q):
        return {"req": lax.rem(z + q + NZ, NZ) * NY + y, "tp": tp}

    def ydev(q):
        return {"req": z * NY + lax.rem(y + q + NY, NY), "tp": tp}

    def tdev(q):
        return {"req": req, "tp": lax.rem(tp + q + NT, NT)}

    partner_dev = {"req": req, "tp": partner}

    def remote(src, dst, ss, rs, dev):
        return pltpu.make_async_remote_copy(
            src_ref=src, dst_ref=dst, send_sem=ss, recv_sem=rs, device_id=dev, device_id_type=MESH
        )

    pending = []

    def go(copy):
        copy.start()
        pending.append(copy)

    def rows2(buf, yb):
        return buf.at[pl.ds(2 * yb, 2)]

    def rows2h(buf, yb, h):
        return buf.at[pl.ds(2 * yb + h, 1)]

    def cols(buf, yb, lo, wide):
        return buf.at[pl.ds(pl.multiple_of(yb * 256, 256), 256), pl.ds(lo, wide)]

    def colsh(buf, yb, h, lo, wide):
        return buf.at[pl.ds(pl.multiple_of(yb * 256 + h * 128, 128), 128), pl.ds(lo, wide)]

    items = [
        (dn, functools.partial(rows2, db), functools.partial(rows2h, db)),
        (uq, functools.partial(rows2, uqb), functools.partial(rows2h, uqb)),
        (ukv, functools.partial(rows2, ukvb), functools.partial(rows2h, ukvb)),
        (wk, lambda b: cols(wkvb, b, 0, 128), lambda b, h: colsh(wkvb, b, h, 0, 128)),
        (wv, lambda b: cols(wkvb, b, 128, 128), lambda b, h: colsh(wkvb, b, h, 128, 128)),
    ]
    for j in range(4):
        items.append((
            wq.at[:, pl.ds(CW * j, CW)],
            lambda b, j=j: cols(wqb, b, CW * j, CW),
            lambda b, h, j=j: colsh(wqb, b, h, CW * j, CW),
        ))
    yl = lax.rem(y + NY - 1, NY)
    yr = lax.rem(y + 1, NY)

    def y_first(i, way):
        src, region, _ = items[i]
        return remote(
            src, region(y), y_ss.at[i, way], y_rs.at[i, way], ydev(1 if way == 0 else -1)
        )

    def y_second(i, way):
        _, _, half = items[i]
        ref = half(yl if way == 0 else yr, way)
        return remote(
            ref, ref, y_ss.at[i, 2 + way], y_rs.at[i, 2 + way], ydev(1 if way == 0 else -1)
        )

    def y_start(i):
        if i < len(items):
            go(y_first(i, 0))
            go(y_first(i, 1))

    def y_pump(i):
        for way in range(2):
            y_first(i, way).wait_recv()
            go(y_second(i, way))
        y_start(i + AHEAD)

    def y_wait(i):
        y_second(i, 0).wait_recv()
        y_second(i, 1).wait_recv()

    barrier = pltpu.get_barrier_semaphore()
    for q in range(1, NZ):
        pl.semaphore_signal(barrier, inc=1, device_id=zdev(q), device_id_type=MESH)
    for q in range(1, NT):
        pl.semaphore_signal(barrier, inc=1, device_id=tdev(q), device_id_type=MESH)
    for q in (1, -1):
        pl.semaphore_signal(barrier, inc=1, device_id=ydev(q), device_id_type=MESH)
    my_rows = pl.ds(pl.multiple_of(tp * 16, 16), 16)
    few_copy = pltpu.make_async_copy(hid.at[my_rows, :], hid16, loc_sem.at[10])
    few_copy.start()
    hid_copy = pltpu.make_async_copy(hid, hidv, loc_sem.at[0])
    hid_copy.start()

    lane = lax.broadcasted_iota(jnp.int32, (TOK, TOK), 1)
    sub = lax.broadcasted_iota(jnp.int32, (TOK, TOK), 0)
    gainf[...] = gain[...].astype(F32)
    tra_c = jnp.transpose(jnp.broadcast_to(tra[...].astype(F32), (TOK, TOK))).astype(jnp.int32)
    held = sas.shape[1]
    sas_r = jnp.broadcast_to(sas[...].astype(F32), (TOK, held))
    slot_c = jnp.sum(
        jnp.where(tra_c[:, :held] == lane[:, :held], sas_r, 0.0), axis=1, keepdims=True
    )
    slot_cm = jnp.broadcast_to(slot_c, (TOK, TOK))
    slot_rm = jnp.transpose(slot_cm).astype(jnp.int32)
    slot_cm = slot_cm.astype(jnp.int32)
    same = (slot_cm >> 1) == (slot_rm >> 1)
    pos_c = jnp.sum(jnp.where(same & (lane < sub), 1.0, 0.0), axis=1, keepdims=True)
    visb[...] = jnp.where(same & (lane <= sub), 1.0, 0.0)
    flat = (slot_cm >> 3) == (slot_rm >> 3)
    rank_r = jnp.sum(jnp.where(flat & (sub < lane), 1.0, 0.0), axis=0, keepdims=True)
    slot_r = slot_rm[0:1, :]
    code_r = slot_r.astype(F32) * 32.0 + rank_r
    meta_s[...] = jnp.broadcast_to(code_r, (8, TOK))
    meta_r[:, 0:TOK] = jnp.broadcast_to(code_r, (8, TOK))
    pos_m = jnp.broadcast_to(pos_c, (TOK, TOK))
    cos = jnp.zeros((TOK, TOK), F32)
    sin = jnp.zeros((TOK, TOK), F32)
    for p in range(8):
        here = pos_m == float(p)
        cos = jnp.where(here, rope[p : p + 1, :], cos)
        sin = jnp.where(here, rope[8 + p : 9 + p, :], sin)
    cosb[...] = cos
    sinb[...] = sin

    pl.semaphore_wait(barrier, 7 + 7 + 2)
    for i in range(AHEAD):
        y_start(i)
    own = []
    for i in range(len(items)):
        src, region, _ = items[i]
        copy = pltpu.make_async_copy(src, region(y), loc_sem.at[1 + i])
        copy.start()
        own.append(copy)

    def inverse_root(ref, rows):
        total = jnp.zeros((16, 128), F32)
        for k in range(8):
            x = ref[rows, pl.ds(k * 1024, 1024)].astype(F32)
            x = x * x
            for m in range(8):
                total = total + x[:, 128 * m : 128 * m + 128]
        return lax.rsqrt(jnp.sum(total, axis=1, keepdims=True) * (1.0 / WIDTH) + 1e-05)

    few_copy.wait()
    s16 = inverse_root(hid16, slice(None))
    for m in range(WIDTH // 128):
        c = slice(128 * m, 128 * m + 128)
        d = 128 * (m % 8)
        asend[m // 8, :, d : d + 128] = (
            hid16[:, c].astype(F32) * s16 * gainf[m : m + 1, :]
        ).astype(BF)

    def a_copy(q):
        k = POS[(-q) % NZ]
        return remote(
            asend.at[lax.rem(z + q, NZ)], act.at[k, my_rows, :],
            a_ss.at[k], a_rs.at[k], zdev(q),
        )

    def m_copy(q):
        k = POS[(-q) % NZ]
        return remote(
            meta_s, meta_r.at[:, pl.ds(k * TOK, TOK)], m_ss.at[k], m_rs.at[k], zdev(q)
        )

    for q in ORDER[1:]:
        go(a_copy(q))
    for q in ORDER[1:]:
        go(m_copy(q))

    hid_copy.wait()

    def stat(i, carry):
        rows = pl.ds(pl.multiple_of(i * 16, 16), 16)
        scale[rows, :] = jnp.broadcast_to(inverse_root(hidv, rows), (16, 128))
        return carry

    lax.fori_loop(0, 8, stat, 0)

    def normed(b, m):
        c = pl.ds(pl.multiple_of(b * PART + 128 * m, 128), 128)
        g = gainf[pl.ds(pl.multiple_of(b * 8, 8), 8), :]
        return (hidv[:, c].astype(F32) * scale[...] * g[m : m + 1, :]).astype(BF)

    target = (slot_rm >> 3) * ROWS + jnp.broadcast_to(rank_r, (TOK, TOK)).astype(jnp.int32)
    sub2 = lax.broadcasted_iota(jnp.int32, (NZ * ROWS, TOK), 0)
    put = jnp.where(
        sub2 == jnp.concatenate([target, target], axis=0), 1.0, 0.0
    ).astype(BF)
    for m in range(8):
        act[0, :, 128 * m : 128 * m + 128] = normed(tp, m)
    rsend[...] = jnp.dot(put, act[0], preferred_element_type=F32).astype(BF)

    def r_block(b):
        return pl.ds(pl.multiple_of(b * ROWS, ROWS), ROWS)

    def r_copy(q):
        k = POS[(-q) % NZ]
        return remote(
            rsend.at[r_block(lax.rem(z + q, NZ)), :], rrecv.at[pl.ds(k * ROWS, ROWS), :],
            r_ss.at[k], r_rs.at[k], zdev(q),
        )

    for q in ORDER[1:]:
        go(r_copy(q))
    rrecv[0:ROWS, :] = rsend[r_block(z), :]
    for m in range(8):
        act[0, :, 128 * m : 128 * m + 128] = normed(z, m)

    def t_rows(q):
        return pl.ds(pl.multiple_of(lax.rem(tp + q + NT, NT) * 16, 16), 16)

    def x_region(g, q, half=None):
        lo, n = GROUPS[g]
        if half is None:
            return act.at[pl.ds(lo, n), t_rows(q), :]
        return act.at[pl.ds(lo, n), t_rows(q), pl.ds(512 * half, 512)]

    def x_first(g, way):
        ref = x_region(g, 0)
        return remote(ref, ref, x_ss.at[g, way], x_rs.at[g, way], tdev(2 if way == 0 else -2))

    def x_second(g, way):
        ref = x_region(g, -2 if way == 0 else 2, way)
        return remote(
            ref, ref, x_ss.at[g, 2 + way], x_rs.at[g, 2 + way], tdev(2 if way == 0 else -2)
        )

    def p_copy(g, k):
        ref = x_region(g, (0, -2, 2, 4)[k])
        return remote(ref, ref, p_ss.at[g, k], p_rs.at[g, k], partner_dev)

    def x_send(g):
        lo, n = GROUPS[g]
        for k in range(lo, lo + n):
            a_copy((-ORDER[k]) % NZ).wait_recv()
        go(x_first(g, 0))
        go(x_first(g, 1))
        go(p_copy(g, 0))

    def x_forward(g):
        for way in range(2):
            x_first(g, way).wait_recv()
            go(x_second(g, way))
            go(p_copy(g, 1 + way))

    def x_last(g):
        x_second(g, 0).wait_recv()
        x_second(g, 1).wait_recv()
        go(p_copy(g, 3))

    x_send(0)
    x_send(1)
    y_pump(0)
    x_send(2)
    y_pump(1)
    x_forward(0)
    y_pump(2)
    x_forward(1)
    x_last(0)

    for q in ORDER[1:]:
        m_copy(q).wait_recv()
    lane2 = lax.broadcasted_iota(jnp.int32, (TOK, NZ * ROWS), 1)
    a8_row = jnp.zeros((8, NZ * ROWS), F32)
    for k in range(NZ):
        code = meta_r[0:8, k * TOK : (k + 1) * TOK]
        code_m = jnp.transpose(jnp.broadcast_to(code[0:1, :], (TOK, TOK)))
        code_c = code_m[:, 0:1].astype(jnp.int32)
        slot_k = code_c >> 5
        want = jnp.where((slot_k >> 3) == z, k * ROWS + (code_c & 31), -1)
        hot = jnp.where(lane2 == want, 1.0, 0.0).astype(BF)
        place[k] = hot
        a8_of[k] = jnp.broadcast_to((slot_k & 7).astype(F32), (TOK, 128))
        a8 = ((code.astype(jnp.int32) >> 5) & 7).astype(F32).astype(BF)
        a8_row = a8_row + jnp.dot(a8, hot, preferred_element_type=F32)

    y_pump(3)
    x_forward(2)
    x_last(1)
    y_pump(4)
    x_last(2)
    for g in range(3):
        for k in range(4):
            p_copy(g, k).wait_recv()

    for copy in own:
        copy.wait()

    def product(c, i):
        a = act[pl.ds(2 * i, 2)].reshape(2 * TOK, PART)
        w = wkvb[...] if c == 0 else wqb[:, CW * (c - 1) : CW * c]
        return jnp.dot(a, w, preferred_element_type=F32).reshape(2, TOK, CW)

    def base(c):
        def tile(i, carry):
            part[c, pl.ds(2 * i, 2)] = product(c, i)
            return carry

        lax.fori_loop(0, NZ // 2, tile, 0)

    y_wait(3)
    y_wait(4)
    base(0)
    y_pump(5)

    y_wait(0)
    for q in ORDER[1:]:
        r_copy(q).wait_recv()
    low_all = lax.dot_general(
        db[...].reshape(8 * 48, PART), rrecv[...], (((1,), (1,)), ((), ())),
        preferred_element_type=F32,
    )
    low_mine = jnp.zeros((48, NZ * ROWS), F32)
    for a in range(8):
        low_mine = low_mine + jnp.where(
            a8_row[0:1, :] == float(a), low_all[48 * a : 48 * a + 48, :], 0.0
        )
    low_s[...] = low_mine.astype(BF)

    def l_copy(q):
        return remote(low_s, low_r.at[q], l_ss.at[q], l_rs.at[q], tdev(q))

    for q in range(1, NT):
        go(l_copy(q))
    y_wait(5)
    base(1)
    y_pump(6)
    for q in range(1, NT):
        l_copy(q).wait_recv()
    low_sum = low_mine
    for q in range(1, NT):
        low_sum = low_sum + low_r[q].astype(F32)
    low_sum = low_sum.astype(BF)
    wide = jnp.concatenate(
        [low_sum[0:16]] * 8 + [low_sum[16:32]] * 8 + [low_sum[32:48]] * 8, axis=0
    )
    which = ((lax.broadcasted_iota(jnp.int32, (TOK, 384), 1) >> 4) & 7).astype(F32)
    for k in range(NZ):
        got = lax.dot_general(
            place[k], wide, (((1,), (1,)), ((), ())), preferred_element_type=F32
        )
        low_l[k] = jnp.where(which == a8_of[k][:, 0:1], got, 0.0).astype(BF)

    y_wait(1)
    y_wait(2)

    def z_copy(c, way, h):
        k = POS[h if way == 0 else NZ - h]
        return remote(
            sendb.at[c, k], recvb.at[c, way, h - 1], z_ss.at[c, way, h - 1],
            z_rs.at[c, way, h - 1], zdev(1 if way == 0 else -1),
        )

    def change(c, i):
        ll = low_l[pl.ds(2 * i, 2)].reshape(2 * TOK, 384)
        if c == 0:
            u_k = ukvb[:, 0:16, :].reshape(128, 128)
            u_v = ukvb[:, 16:32, :].reshape(128, 128)
            d = jnp.concatenate(
                [
                    jnp.dot(ll[:, 128:256], u_k, preferred_element_type=F32),
                    jnp.dot(ll[:, 256:384], u_v, preferred_element_type=F32),
                ],
                axis=1,
            )
        else:
            u_q = uqb[:, :, CW * (c - 1) : CW * c].reshape(128, CW)
            d = jnp.dot(ll[:, 0:128], u_q, preferred_element_type=F32)
        return (0.5 * d.astype(BF).astype(F32)).reshape(2, TOK, CW)

    def complete(c):
        def tile(i, carry):
            here = part[c, pl.ds(2 * i, 2)] if c < 2 else product(c, i)
            part[c, pl.ds(2 * i, 2)] = here + change(c, i)
            return carry

        lax.fori_loop(0, NZ // 2, tile, 0)

    def ring(c, h):
        for way in range(2):
            if h > longest(c, way):
                continue
            k = POS[h if way == 0 else NZ - h]
            total = part[c, k]
            if h + 1 <= longest(c, way):
                z_copy(c, way, h + 1).wait_recv()
                total = total + recvb[c, way, h].astype(F32)
            sendb[c, k] = total.astype(BF)
            go(z_copy(c, way, h))

    for c in range(2):
        complete(c)
        ring(c, 4)
    y_pump(7)
    ring(0, 3)
    ring(1, 3)
    for c in range(2, CHUNKS):
        y_wait(4 + c)
        complete(c)
        ring(c, 4)
        if c == 2:
            y_pump(8)
    for c in range(2, CHUNKS):
        ring(c, 3)
    for h in (2, 1):
        for c in range(CHUNKS):
            ring(c, h)

    def final(c):
        z_copy(c, 0, 1).wait_recv()
        z_copy(c, 1, 1).wait_recv()
        return part[c, 0] + recvb[c, 0, 0].astype(F32) + recvb[c, 1, 0].astype(F32)

    cos = cosb[...]
    sin = sinb[...]

    def turn(u):
        return u * cos + pltpu.roll(u, HEAD // 2, 1) * sin

    kv = final(0)
    keys = turn(kv[:, 0:HEAD]).astype(BF)
    values = kv[:, HEAD:].astype(BF)
    kout[...] = keys
    vout[...] = values
    seen = visb[...] > 0.5
    root = float(np.float32(1.0) / np.sqrt(np.float32(HEAD)))
    for c in range(1, CHUNKS):
        both = final(c)
        for i in range(2):
            query = turn(both[:, HEAD * i : HEAD * (i + 1)]).astype(BF)
            scores = lax.dot_general(
                query, keys, (((1,), (1,)), ((), ())), preferred_element_type=F32
            ) * root
            scores = jnp.where(seen, scores, -1e30)
            raised = jnp.exp(scores - jnp.max(scores, axis=1, keepdims=True))
            weights = (raised / jnp.sum(raised, axis=1, keepdims=True)).astype(BF)
            lo = CW * (c - 1) + HEAD * i
            ctx[:, lo : lo + HEAD] = jnp.dot(
                weights, values, preferred_element_type=F32
            ).astype(BF)

    for copy in pending:
        copy.wait_send()


def forward(a, b, c, ao, bo, co):
    ao[...] = a[...]
    bo[...] = b[...]
    co[...] = c[...]


def rope_table():
    half = HEAD // 2
    freq = np.float32(10000.0) ** (-(np.arange(half, dtype=np.float32) * np.float32(2.0) / HEAD))
    angle = np.arange(8, dtype=np.float32)[:, None] * freq[None, :].astype(np.float32)
    cos = np.cos(angle).astype(np.float32)
    sin = np.sin(angle).astype(np.float32)
    return np.concatenate(
        [np.concatenate([cos, cos], axis=1), np.concatenate([-sin, sin], axis=1)], axis=0
    )


def per_device(hidden, gain, wq, wk, wv, down, up_q, up_kv, adapter, storage):
    any_spec = pl.BlockSpec(memory_space=pl.ANY)
    vmem = pl.BlockSpec(memory_space=pltpu.VMEM)
    dma = pltpu.SemaphoreType.DMA
    count = storage.shape[0]
    call = pl.pallas_call(
        body,
        out_shape=(
            jax.ShapeDtypeStruct((TOK, PART), BF),
            jax.ShapeDtypeStruct((TOK, HEAD), BF),
            jax.ShapeDtypeStruct((TOK, HEAD), BF),
        ),
        in_specs=[any_spec, vmem, vmem, vmem, vmem] + [any_spec] * 6,
        out_specs=(vmem, vmem, vmem),
        scratch_shapes=[
            pltpu.VMEM((TOK, WIDTH), BF),
            pltpu.VMEM((16, WIDTH), BF),
            pltpu.VMEM((WIDTH // 128, 128), F32),
            pltpu.VMEM((TOK, 128), F32),
            pltpu.VMEM((NZ, TOK, PART), BF),
            pltpu.VMEM((NZ, 16, PART), BF),
            pltpu.VMEM((8, TOK), F32),
            pltpu.VMEM((8, NZ * TOK), F32),
            pltpu.VMEM((NZ * ROWS, PART), BF),
            pltpu.VMEM((NZ * ROWS, PART), BF),
            pltpu.VMEM((PART, PART), BF),
            pltpu.VMEM((PART, CW), BF),
            pltpu.VMEM((8, 48, PART), BF),
            pltpu.VMEM((8, 16, PART), BF),
            pltpu.VMEM((8, 32, HEAD), BF),
            pltpu.VMEM((NZ, TOK, NZ * ROWS), BF),
            pltpu.VMEM((NZ, TOK, 128), F32),
            pltpu.VMEM((48, NZ * ROWS), BF),
            pltpu.VMEM((NT, 48, NZ * ROWS), BF),
            pltpu.VMEM((NZ, TOK, 384), BF),
            pltpu.VMEM((CHUNKS, NZ, TOK, CW), F32),
            pltpu.VMEM((CHUNKS, NZ, TOK, CW), BF),
            pltpu.VMEM((CHUNKS, 2, 4, TOK, CW), BF),
            pltpu.VMEM((TOK, TOK), F32),
            pltpu.VMEM((TOK, TOK), F32),
            pltpu.VMEM((TOK, TOK), F32),
            dma((11,)),
            dma((9, 4)), dma((9, 4)),
            dma((NZ,)), dma((NZ,)),
            dma((NZ,)), dma((NZ,)),
            dma((NZ,)), dma((NZ,)),
            dma((3, 4)), dma((3, 4)),
            dma((3, 4)), dma((3, 4)),
            dma((NT,)), dma((NT,)),
            dma((CHUNKS, 2, 4)), dma((CHUNKS, 2, 4)),
        ],
        compiler_params=pltpu.CompilerParams(
            collective_id=0, has_side_effects=True, vmem_limit_bytes=60 * 1024 * 1024
        ),
    )
    outs = call(
        hidden,
        gain.reshape(WIDTH // 128, 128),
        adapter.reshape(1, TOK),
        storage.reshape(1, count),
        jnp.asarray(rope_table()),
        wq, wk, wv, down, up_q, up_kv,
    )
    return pl.pallas_call(
        forward,
        out_shape=tuple(jax.ShapeDtypeStruct(o.shape, o.dtype) for o in outs),
        in_specs=[vmem] * 3,
        out_specs=(vmem,) * 3,
    )(*outs)


def solution(mesh):
    in_specs = (
        P("req", None),
        P(),
        P("req", "tp"),
        P("req", "tp"),
        P("req", "tp"),
        P("req", None, "tp"),
        P("req", None, "tp"),
        P("req", None, "tp"),
        P("req"),
        P(),
    )
    out_specs = (P("req", "tp"), P("req", "tp"), P("req", "tp"))
    return jax.shard_map(
        per_device, mesh=mesh, in_specs=in_specs, out_specs=out_specs, check_vma=False
    )
```

```python
import functools

import jax
import jax.numpy as jnp
import numpy as np
from jax import lax
from jax.experimental import pallas as pl
from jax.experimental.pallas import tpu as pltpu
from jax.sharding import PartitionSpec as P

MESH = pl.DeviceIdType.MESH
HEAD = 128
NY = 4
NZ = 8
NT = 8
TOK = 128
WIDTH = 8192
PART = 1024
CW = 256
ROWS = 32
CHUNKS = 5
BF = jnp.bfloat16
F32 = jnp.float32
ORDER = (0, 1, 7, 2, 6, 3, 5, 4)
POS = tuple(ORDER.index(r) for r in range(NZ))
GROUPS = ((1, 2), (3, 2), (5, 3))
FAR_FIRST = (7, 6, 5, 4, 3, 2, 1)
AHEAD = 3


def longest(c, way):
    return 4 if way == (1 if c % 2 == 0 else 0) else 3


def body(
    hid, gain_h, tra_h, sas_h, rope_h, wq, wk, wv, dn, uq, ukv,
    ctx, kout, vout,
    gain, tra, sas, rope, hidv, hid16, gainf, scale, act, asend, meta_s, meta_r, rsend, rrecv,
    wqb, wkvb, db, uqb, ukvb,
    place, a8_of, low_s, low_r, low_l, part, sendb, recvb, cosb, sinb, visb,
    loc_sem, y_ss, y_rs, a_ss, a_rs, m_ss, m_rs, r_ss, r_rs,
    x_ss, x_rs, p_ss, p_rs, l_ss, l_rs, z_ss, z_rs,
):
    req = lax.axis_index("req")
    tp = lax.axis_index("tp")
    z = req // NY
    y = req % NY
    core = tp % 2
    partner = tp + 1 - 2 * core

    def zdev(q):
        return {"req": lax.rem(z + q + NZ, NZ) * NY + y, "tp": tp}

    def ydev(q):
        return {"req": z * NY + lax.rem(y + q + NY, NY), "tp": tp}

    def tdev(q):
        return {"req": req, "tp": lax.rem(tp + q + NT, NT)}

    partner_dev = {"req": req, "tp": partner}

    def remote(src, dst, ss, rs, dev):
        return pltpu.make_async_remote_copy(
            src_ref=src, dst_ref=dst, send_sem=ss, recv_sem=rs, device_id=dev, device_id_type=MESH
        )

    pending = []

    def go(copy):
        copy.start()
        pending.append(copy)

    def rows2(buf, yb):
        return buf.at[pl.ds(2 * yb, 2)]

    def rows2h(buf, yb, h):
        return buf.at[pl.ds(2 * yb + h, 1)]

    def cols(buf, yb, lo, wide):
        return buf.at[pl.ds(pl.multiple_of(yb * 256, 256), 256), pl.ds(lo, wide)]

    def colsh(buf, yb, h, lo, wide):
        return buf.at[pl.ds(pl.multiple_of(yb * 256 + h * 128, 128), 128), pl.ds(lo, wide)]

    items = [
        (dn, functools.partial(rows2, db), functools.partial(rows2h, db)),
        (wk, lambda b: cols(wkvb, b, 0, 128), lambda b, h: colsh(wkvb, b, h, 0, 128)),
        (wv, lambda b: cols(wkvb, b, 128, 128), lambda b, h: colsh(wkvb, b, h, 128, 128)),
        (uq, functools.partial(rows2, uqb), functools.partial(rows2h, uqb)),
        (ukv, functools.partial(rows2, ukvb), functools.partial(rows2h, ukvb)),
    ]
    for j in range(4):
        items.append((
            wq.at[:, pl.ds(CW * j, CW)],
            lambda b, j=j: cols(wqb, b, CW * j, CW),
            lambda b, h, j=j: colsh(wqb, b, h, CW * j, CW),
        ))
    yl = lax.rem(y + NY - 1, NY)
    yr = lax.rem(y + 1, NY)

    def y_first(i, way):
        src, region, _ = items[i]
        return remote(
            src, region(y), y_ss.at[i, way], y_rs.at[i, way], ydev(1 if way == 0 else -1)
        )

    def y_second(i, way):
        _, _, half = items[i]
        ref = half(yl if way == 0 else yr, way)
        return remote(
            ref, ref, y_ss.at[i, 2 + way], y_rs.at[i, 2 + way], ydev(1 if way == 0 else -1)
        )

    def y_start(i):
        if i < len(items):
            go(y_first(i, 0))
            go(y_first(i, 1))

    def y_pump(i):
        for way in range(2):
            y_first(i, way).wait_recv()
            go(y_second(i, way))
        y_start(i + AHEAD)

    def y_wait(i):
        y_second(i, 0).wait_recv()
        y_second(i, 1).wait_recv()

    barrier = pltpu.get_barrier_semaphore()
    for q in range(1, NZ):
        pl.semaphore_signal(barrier, inc=1, device_id=zdev(q), device_id_type=MESH)
    for q in range(1, NT):
        pl.semaphore_signal(barrier, inc=1, device_id=tdev(q), device_id_type=MESH)
    for q in (1, -1):
        pl.semaphore_signal(barrier, inc=1, device_id=ydev(q), device_id_type=MESH)
    my_rows = pl.ds(pl.multiple_of(tp * 16, 16), 16)
    few_copy = pltpu.make_async_copy(hid.at[my_rows, :], hid16, loc_sem.at[10])
    few_copy.start()
    small = []
    for i, (src, dst) in enumerate(((gain_h, gain), (tra_h, tra), (sas_h, sas), (rope_h, rope))):
        copy = pltpu.make_async_copy(src, dst, loc_sem.at[11 + i])
        copy.start()
        small.append(copy)
    hid_copy = pltpu.make_async_copy(hid, hidv, loc_sem.at[0])
    hid_copy.start()

    pl.semaphore_wait(barrier, 7 + 7 + 2)
    for i in range(AHEAD):
        y_start(i)
    own = []
    for i in range(len(items)):
        src, region, _ = items[i]
        copy = pltpu.make_async_copy(src, region(y), loc_sem.at[1 + i])
        copy.start()
        own.append(copy)

    def inverse_root(ref, rows):
        total = jnp.zeros((16, 128), F32)
        for k in range(8):
            x = ref[rows, pl.ds(k * 1024, 1024)].astype(F32)
            x = x * x
            for m in range(8):
                total = total + x[:, 128 * m : 128 * m + 128]
        return lax.rsqrt(jnp.sum(total, axis=1, keepdims=True) * (1.0 / WIDTH) + 1e-05)

    few_copy.wait()
    for copy in small:
        copy.wait()
    gainf[...] = gain[...].astype(F32)
    s16 = inverse_root(hid16, slice(None))
    for m in range(WIDTH // 128):
        c = slice(128 * m, 128 * m + 128)
        d = 128 * (m % 8)
        asend[m // 8, :, d : d + 128] = (
            hid16[:, c].astype(F32) * s16 * gainf[m : m + 1, :]
        ).astype(BF)

    def a_copy(q):
        k = POS[(-q) % NZ]
        return remote(
            asend.at[lax.rem(z + q, NZ)], act.at[k, my_rows, :],
            a_ss.at[k], a_rs.at[k], zdev(q),
        )

    def m_copy(q):
        k = POS[(-q) % NZ]
        return remote(
            meta_s, meta_r.at[:, pl.ds(k * TOK, TOK)], m_ss.at[k], m_rs.at[k], zdev(q)
        )

    for k in FAR_FIRST:
        go(a_copy((-ORDER[k]) % NZ))

    lane = lax.broadcasted_iota(jnp.int32, (TOK, TOK), 1)
    sub = lax.broadcasted_iota(jnp.int32, (TOK, TOK), 0)
    tra_c = jnp.transpose(jnp.broadcast_to(tra[...].astype(F32), (TOK, TOK))).astype(jnp.int32)
    held = sas.shape[1]
    sas_r = jnp.broadcast_to(sas[...].astype(F32), (TOK, held))
    slot_c = jnp.sum(
        jnp.where(tra_c[:, :held] == lane[:, :held], sas_r, 0.0), axis=1, keepdims=True
    )
    slot_cm = jnp.broadcast_to(slot_c, (TOK, TOK))
    slot_rm = jnp.transpose(slot_cm).astype(jnp.int32)
    slot_cm = slot_cm.astype(jnp.int32)
    same = (slot_cm >> 1) == (slot_rm >> 1)
    pos_c = jnp.sum(jnp.where(same & (lane < sub), 1.0, 0.0), axis=1, keepdims=True)
    visb[...] = jnp.where(same & (lane <= sub), 1.0, 0.0)
    flat = (slot_cm >> 3) == (slot_rm >> 3)
    rank_r = jnp.sum(jnp.where(flat & (sub < lane), 1.0, 0.0), axis=0, keepdims=True)
    slot_r = slot_rm[0:1, :]
    code_r = slot_r.astype(F32) * 32.0 + rank_r
    meta_s[...] = jnp.broadcast_to(code_r, (8, TOK))
    meta_r[:, 0:TOK] = jnp.broadcast_to(code_r, (8, TOK))
    for k in FAR_FIRST:
        go(m_copy((-ORDER[k]) % NZ))
    hid_copy.wait()

    def stat(i, carry):
        rows = pl.ds(pl.multiple_of(i * 16, 16), 16)
        scale[rows, :] = jnp.broadcast_to(inverse_root(hidv, rows), (16, 128))
        return carry

    lax.fori_loop(0, 8, stat, 0)

    def normed(b, m):
        c = pl.ds(pl.multiple_of(b * PART + 128 * m, 128), 128)
        g = gainf[pl.ds(pl.multiple_of(b * 8, 8), 8), :]
        return (hidv[:, c].astype(F32) * scale[...] * g[m : m + 1, :]).astype(BF)

    target = (slot_rm >> 3) * ROWS + jnp.broadcast_to(rank_r, (TOK, TOK)).astype(jnp.int32)
    sub2 = lax.broadcasted_iota(jnp.int32, (NZ * ROWS, TOK), 0)
    put = jnp.where(
        sub2 == jnp.concatenate([target, target], axis=0), 1.0, 0.0
    ).astype(BF)
    for m in range(8):
        act[0, :, 128 * m : 128 * m + 128] = normed(tp, m)
    rsend[...] = jnp.dot(put, act[0], preferred_element_type=F32).astype(BF)

    def r_block(b):
        return pl.ds(pl.multiple_of(b * ROWS, ROWS), ROWS)

    def r_copy(q):
        k = POS[(-q) % NZ]
        return remote(
            rsend.at[r_block(lax.rem(z + q, NZ)), :], rrecv.at[pl.ds(k * ROWS, ROWS), :],
            r_ss.at[k], r_rs.at[k], zdev(q),
        )

    for k in FAR_FIRST:
        go(r_copy((-ORDER[k]) % NZ))
    rrecv[0:ROWS, :] = rsend[r_block(z), :]
    for m in range(8):
        act[0, :, 128 * m : 128 * m + 128] = normed(z, m)

    def t_rows(q):
        return pl.ds(pl.multiple_of(lax.rem(tp + q + NT, NT) * 16, 16), 16)

    def x_region(g, q, half=None):
        lo, n = GROUPS[g]
        if half is None:
            return act.at[pl.ds(lo, n), t_rows(q), :]
        return act.at[pl.ds(lo, n), t_rows(q), pl.ds(512 * half, 512)]

    def x_first(g, way):
        ref = x_region(g, 0)
        return remote(ref, ref, x_ss.at[g, way], x_rs.at[g, way], tdev(2 if way == 0 else -2))

    def x_second(g, way):
        ref = x_region(g, -2 if way == 0 else 2, way)
        return remote(
            ref, ref, x_ss.at[g, 2 + way], x_rs.at[g, 2 + way], tdev(2 if way == 0 else -2)
        )

    def p_copy(g, k):
        ref = x_region(g, (0, -2, 2, 4)[k])
        return remote(ref, ref, p_ss.at[g, k], p_rs.at[g, k], partner_dev)

    def x_send(g):
        lo, n = GROUPS[g]
        for k in range(lo, lo + n):
            a_copy((-ORDER[k]) % NZ).wait_recv()
        go(x_first(g, 0))
        go(x_first(g, 1))
        go(p_copy(g, 0))

    def x_forward(g):
        for way in range(2):
            x_first(g, way).wait_recv()
            go(x_second(g, way))
            go(p_copy(g, 1 + way))

    def x_last(g):
        x_second(g, 0).wait_recv()
        x_second(g, 1).wait_recv()
        go(p_copy(g, 3))

    x_send(2)
    y_pump(0)
    x_send(1)
    y_pump(1)
    x_send(0)
    x_forward(2)
    y_pump(2)
    x_forward(1)
    x_last(2)

    for q in ORDER[1:]:
        m_copy(q).wait_recv()
    a8_row = [jnp.zeros((8, TOK), F32) for _ in range(2)]
    for k in range(NZ):
        code = meta_r[0:8, k * TOK : (k + 1) * TOK]
        code_m = jnp.transpose(jnp.broadcast_to(code[0:1, :], (TOK, TOK))).astype(jnp.int32)
        slot_k = code_m >> 5
        want = jnp.where((slot_k >> 3) == z, (k % 4) * ROWS + (code_m & 31), -1)
        hot = jnp.where(lane == want, 1.0, 0.0).astype(BF)
        place[k] = hot
        a8_of[k] = (slot_k & 7).astype(F32)
        a8 = ((code.astype(jnp.int32) >> 5) & 7).astype(F32).astype(BF)
        a8_row[k // 4] = a8_row[k // 4] + jnp.dot(a8, hot, preferred_element_type=F32)

    y_pump(3)
    x_forward(0)
    x_last(1)
    y_pump(4)
    x_last(0)

    low_mine = [None, None]

    def l_copy(g, q):
        return remote(low_s.at[g], low_r.at[g, q], l_ss.at[g, q], l_rs.at[g, q], tdev(q))

    def low_products(g):
        for k in range(max(1, 4 * g), 4 * g + 4):
            r_copy((-ORDER[k]) % NZ).wait_recv()
        low_all = lax.dot_general(
            db[...].reshape(8 * 48, PART), rrecv[TOK * g : TOK * (g + 1), :],
            (((1,), (1,)), ((), ())), preferred_element_type=F32,
        )
        mine = jnp.zeros((48, TOK), F32)
        for a in range(8):
            mine = mine + jnp.where(
                a8_row[g][0:1, :] == float(a), low_all[48 * a : 48 * a + 48, :], 0.0
            )
        low_mine[g] = mine
        low_s[g] = mine.astype(BF)
        for q in range(1, NT):
            go(l_copy(g, q))

    which = ((lax.broadcasted_iota(jnp.int32, (TOK, 384), 1) >> 4) & 7).astype(F32)

    def low_table(g):
        total = low_mine[g]
        for q in range(1, NT):
            l_copy(g, q).wait_recv()
            total = total + low_r[g, q].astype(F32)
        total = total.astype(BF)
        wide = jnp.concatenate(
            [total[0:16]] * 8 + [total[16:32]] * 8 + [total[32:48]] * 8, axis=0
        )
        for k in range(4 * g, 4 * g + 4):
            got = lax.dot_general(
                place[k], wide, (((1,), (1,)), ((), ())), preferred_element_type=F32
            )
            low_l[k] = jnp.where(which == a8_of[k][:, 0:1], got, 0.0).astype(BF)

    def product(c, i):
        a = act[pl.ds(2 * i, 2)].reshape(2 * TOK, PART)
        w = wkvb[...] if c == 0 else wqb[:, CW * (c - 1) : CW * c]
        return jnp.dot(a, w, preferred_element_type=F32).reshape(2, TOK, CW)

    def base(c, g):
        def tile(i, carry):
            part[c, pl.ds(2 * i, 2)] = product(c, i)
            return carry

        lax.fori_loop(2 * g, 2 * g + 2, tile, 0)

    for copy in own:
        copy.wait()
    y_wait(0)
    low_products(1)
    y_pump(5)
    for g in range(3):
        for k in range(4):
            p_copy(g, k).wait_recv()
    y_wait(1)
    y_wait(2)
    base(0, 1)
    low_products(0)
    base(0, 0)
    low_table(1)
    y_wait(3)
    y_wait(4)

    def z_copy(c, way, h):
        k = POS[h if way == 0 else NZ - h]
        return remote(
            sendb.at[c, k], recvb.at[c, way, h - 1], z_ss.at[c, way, h - 1],
            z_rs.at[c, way, h - 1], zdev(1 if way == 0 else -1),
        )

    def change(c, i):
        ll = low_l[pl.ds(2 * i, 2)].reshape(2 * TOK, 384)
        if c == 0:
            u_k = ukvb[:, 0:16, :].reshape(128, 128)
            u_v = ukvb[:, 16:32, :].reshape(128, 128)
            d = jnp.concatenate(
                [
                    jnp.dot(ll[:, 128:256], u_k, preferred_element_type=F32),
                    jnp.dot(ll[:, 256:384], u_v, preferred_element_type=F32),
                ],
                axis=1,
            )
        else:
            u_q = uqb[:, :, CW * (c - 1) : CW * c].reshape(128, CW)
            d = jnp.dot(ll[:, 0:128], u_q, preferred_element_type=F32)
        return (0.5 * d.astype(BF).astype(F32)).reshape(2, TOK, CW)

    def complete(c, g):
        def tile(i, carry):
            here = product(c, i) if c > 0 else part[c, pl.ds(2 * i, 2)]
            part[c, pl.ds(2 * i, 2)] = here + change(c, i)
            return carry

        lax.fori_loop(2 * g, 2 * g + 2, tile, 0)

    def ring(c, h):
        for way in range(2):
            if h > longest(c, way):
                continue
            k = POS[h if way == 0 else NZ - h]
            total = part[c, k]
            if h + 1 <= longest(c, way):
                z_copy(c, way, h + 1).wait_recv()
                total = total + recvb[c, way, h].astype(F32)
            sendb[c, k] = total.astype(BF)
            go(z_copy(c, way, h))

    complete(0, 1)
    ring(0, 4)
    y_pump(6)
    low_table(0)
    y_pump(7)
    y_wait(5)
    complete(1, 1)
    ring(1, 4)
    complete(0, 0)
    ring(0, 3)
    y_pump(8)
    complete(1, 0)
    ring(1, 3)
    for c in range(2, CHUNKS):
        y_wait(4 + c)
        complete(c, 1)
        ring(c, 4)
    for c in range(2, CHUNKS):
        ring(c, 3)
        complete(c, 0)
    for c in range(CHUNKS):
        ring(c, 2)
    pos_m = jnp.broadcast_to(pos_c, (TOK, TOK))
    cos = jnp.zeros((TOK, TOK), F32)
    sin = jnp.zeros((TOK, TOK), F32)
    for p in range(8):
        here = pos_m == float(p)
        cos = jnp.where(here, rope[p : p + 1, :], cos)
        sin = jnp.where(here, rope[8 + p : 9 + p, :], sin)
    cosb[...] = cos
    sinb[...] = sin

    for c in range(CHUNKS):
        ring(c, 1)

    def final(c):
        z_copy(c, 0, 1).wait_recv()
        z_copy(c, 1, 1).wait_recv()
        return part[c, 0] + recvb[c, 0, 0].astype(F32) + recvb[c, 1, 0].astype(F32)

    cos = cosb[...]
    sin = sinb[...]

    def turn(u):
        return u * cos + pltpu.roll(u, HEAD // 2, 1) * sin

    kv = final(0)
    keys = turn(kv[:, 0:HEAD]).astype(BF)
    values = kv[:, HEAD:].astype(BF)
    kout[...] = keys
    vout[...] = values
    seen = visb[...] > 0.5
    root = float(np.float32(1.0) / np.sqrt(np.float32(HEAD)))
    for c in range(1, CHUNKS):
        both = final(c)
        for i in range(2):
            query = turn(both[:, HEAD * i : HEAD * (i + 1)]).astype(BF)
            scores = lax.dot_general(
                query, keys, (((1,), (1,)), ((), ())), preferred_element_type=F32
            ) * root
            scores = jnp.where(seen, scores, -1e30)
            raised = jnp.exp(scores - jnp.max(scores, axis=1, keepdims=True))
            weights = (raised / jnp.sum(raised, axis=1, keepdims=True)).astype(BF)
            lo = CW * (c - 1) + HEAD * i
            ctx[:, lo : lo + HEAD] = jnp.dot(
                weights, values, preferred_element_type=F32
            ).astype(BF)

    for copy in pending:
        copy.wait_send()


def forward(a, b, c, ao, bo, co):
    ao[...] = a[...]
    bo[...] = b[...]
    co[...] = c[...]


def rope_table():
    half = HEAD // 2
    freq = np.float32(10000.0) ** (-(np.arange(half, dtype=np.float32) * np.float32(2.0) / HEAD))
    angle = np.arange(8, dtype=np.float32)[:, None] * freq[None, :].astype(np.float32)
    cos = np.cos(angle).astype(np.float32)
    sin = np.sin(angle).astype(np.float32)
    return np.concatenate(
        [np.concatenate([cos, cos], axis=1), np.concatenate([-sin, sin], axis=1)], axis=0
    )


def per_device(hidden, gain, wq, wk, wv, down, up_q, up_kv, adapter, storage):
    any_spec = pl.BlockSpec(memory_space=pl.ANY)
    vmem = pl.BlockSpec(memory_space=pltpu.VMEM)
    dma = pltpu.SemaphoreType.DMA
    count = storage.shape[0]
    call = pl.pallas_call(
        body,
        out_shape=(
            jax.ShapeDtypeStruct((TOK, PART), BF),
            jax.ShapeDtypeStruct((TOK, HEAD), BF),
            jax.ShapeDtypeStruct((TOK, HEAD), BF),
        ),
        in_specs=[any_spec] * 11,
        out_specs=(vmem, vmem, vmem),
        scratch_shapes=[
            pltpu.VMEM((WIDTH // 128, 128), BF),
            pltpu.VMEM((1, TOK), jnp.int32),
            pltpu.VMEM((1, count), jnp.int32),
            pltpu.VMEM((16, 128), F32),
            pltpu.VMEM((TOK, WIDTH), BF),
            pltpu.VMEM((16, WIDTH), BF),
            pltpu.VMEM((WIDTH // 128, 128), F32),
            pltpu.VMEM((TOK, 128), F32),
            pltpu.VMEM((NZ, TOK, PART), BF),
            pltpu.VMEM((NZ, 16, PART), BF),
            pltpu.VMEM((8, TOK), F32),
            pltpu.VMEM((8, NZ * TOK), F32),
            pltpu.VMEM((NZ * ROWS, PART), BF),
            pltpu.VMEM((NZ * ROWS, PART), BF),
            pltpu.VMEM((PART, PART), BF),
            pltpu.VMEM((PART, CW), BF),
            pltpu.VMEM((8, 48, PART), BF),
            pltpu.VMEM((8, 16, PART), BF),
            pltpu.VMEM((8, 32, HEAD), BF),
            pltpu.VMEM((NZ, TOK, TOK), BF),
            pltpu.VMEM((NZ, TOK, 128), F32),
            pltpu.VMEM((2, 48, TOK), BF),
            pltpu.VMEM((2, NT, 48, TOK), BF),
            pltpu.VMEM((NZ, TOK, 384), BF),
            pltpu.VMEM((CHUNKS, NZ, TOK, CW), F32),
            pltpu.VMEM((CHUNKS, NZ, TOK, CW), BF),
            pltpu.VMEM((CHUNKS, 2, 4, TOK, CW), BF),
            pltpu.VMEM((TOK, TOK), F32),
            pltpu.VMEM((TOK, TOK), F32),
            pltpu.VMEM((TOK, TOK), F32),
            dma((15,)),
            dma((9, 4)), dma((9, 4)),
            dma((NZ,)), dma((NZ,)),
            dma((NZ,)), dma((NZ,)),
            dma((NZ,)), dma((NZ,)),
            dma((3, 4)), dma((3, 4)),
            dma((3, 4)), dma((3, 4)),
            dma((2, NT)), dma((2, NT)),
            dma((CHUNKS, 2, 4)), dma((CHUNKS, 2, 4)),
        ],
        compiler_params=pltpu.CompilerParams(
            collective_id=0, has_side_effects=True, vmem_limit_bytes=60 * 1024 * 1024
        ),
    )
    outs = call(
        hidden,
        gain.reshape(WIDTH // 128, 128),
        adapter.reshape(1, TOK),
        storage.reshape(1, count),
        jnp.asarray(rope_table()),
        wq, wk, wv, down, up_q, up_kv,
    )
    return pl.pallas_call(
        forward,
        out_shape=tuple(jax.ShapeDtypeStruct(o.shape, o.dtype) for o in outs),
        in_specs=[vmem] * 3,
        out_specs=(vmem,) * 3,
    )(*outs)


def solution(mesh):
    in_specs = (
        P("req", None),
        P(),
        P("req", "tp"),
        P("req", "tp"),
        P("req", "tp"),
        P("req", None, "tp"),
        P("req", None, "tp"),
        P("req", None, "tp"),
        P("req"),
        P(),
    )
    out_specs = (P("req", "tp"), P("req", "tp"), P("req", "tp"))
    return jax.shard_map(
        per_device, mesh=mesh, in_specs=in_specs, out_specs=out_specs, check_vma=False
    )
```

```python
import functools

import jax
import jax.numpy as jnp
import numpy as np
from jax import lax
from jax.experimental import pallas as pl
from jax.experimental.pallas import tpu as pltpu
from jax.sharding import PartitionSpec as P

MESH = pl.DeviceIdType.MESH
HEAD = 128
NY = 4
NZ = 8
NT = 8
TOK = 128
WIDTH = 8192
PART = 1024
CW = 256
ROWS = 32
CHUNKS = 5
BF = jnp.bfloat16
F32 = jnp.float32
ORDER = (0, 1, 7, 2, 6, 3, 5, 4)
POS = tuple(ORDER.index(r) for r in range(NZ))
GROUPS = ((1, 2), (3, 2), (5, 3))
FAR_FIRST = (7, 6, 5, 4, 3, 2, 1)
AHEAD = 3


def longest(c, way):
    return 4 if way == (1 if c % 2 == 0 else 0) else 3


def body(
    hid, gain_h, tra_h, sas_h, rope_h, wq, wk, wv, dn, uq, ukv,
    ctx, kout, vout,
    gain, tra, sas, rope, hidv, hid16, gainf, scale, act, asend, meta_s, meta_r, rsend, rrecv,
    wqb, wkvb, db, uqb, ukvb,
    place, a8_of, low_s, low_r, low_l, part, sendb, recvb, cosb, sinb, visb,
    loc_sem, y_ss, y_rs, a_ss, a_rs, m_ss, m_rs, r_ss, r_rs,
    x_ss, x_rs, p_ss, p_rs, l_ss, l_rs, z_ss, z_rs,
):
    req = lax.axis_index("req")
    tp = lax.axis_index("tp")
    z = req // NY
    y = req % NY
    core = tp % 2
    partner = tp + 1 - 2 * core

    def zdev(q):
        return {"req": lax.rem(z + q + NZ, NZ) * NY + y, "tp": tp}

    def ydev(q):
        return {"req": z * NY + lax.rem(y + q + NY, NY), "tp": tp}

    def tdev(q):
        return {"req": req, "tp": lax.rem(tp + q + NT, NT)}

    partner_dev = {"req": req, "tp": partner}

    def remote(src, dst, ss, rs, dev):
        return pltpu.make_async_remote_copy(
            src_ref=src, dst_ref=dst, send_sem=ss, recv_sem=rs, device_id=dev, device_id_type=MESH
        )

    pending = []

    def go(copy):
        copy.start()
        pending.append(copy)

    def rows2(buf, yb):
        return buf.at[pl.ds(2 * yb, 2)]

    def rows2h(buf, yb, h):
        return buf.at[pl.ds(2 * yb + h, 1)]

    def cols(buf, yb, lo, wide):
        return buf.at[pl.ds(pl.multiple_of(yb * 256, 256), 256), pl.ds(lo, wide)]

    def colsh(buf, yb, h, lo, wide):
        return buf.at[pl.ds(pl.multiple_of(yb * 256 + h * 128, 128), 128), pl.ds(lo, wide)]

    items = [
        (dn, functools.partial(rows2, db), functools.partial(rows2h, db)),
        (wk, lambda b: cols(wkvb, b, 0, 128), lambda b, h: colsh(wkvb, b, h, 0, 128)),
        (wv, lambda b: cols(wkvb, b, 128, 128), lambda b, h: colsh(wkvb, b, h, 128, 128)),
        (uq, functools.partial(rows2, uqb), functools.partial(rows2h, uqb)),
        (ukv, functools.partial(rows2, ukvb), functools.partial(rows2h, ukvb)),
    ]
    for j in range(4):
        items.append((
            wq.at[:, pl.ds(CW * j, CW)],
            lambda b, j=j: cols(wqb, b, CW * j, CW),
            lambda b, h, j=j: colsh(wqb, b, h, CW * j, CW),
        ))
    yl = lax.rem(y + NY - 1, NY)
    yr = lax.rem(y + 1, NY)

    def y_first(i, way):
        src, region, _ = items[i]
        return remote(
            src, region(y), y_ss.at[i, way], y_rs.at[i, way], ydev(1 if way == 0 else -1)
        )

    def y_second(i, way):
        _, _, half = items[i]
        ref = half(yl if way == 0 else yr, way)
        return remote(
            ref, ref, y_ss.at[i, 2 + way], y_rs.at[i, 2 + way], ydev(1 if way == 0 else -1)
        )

    def y_start(i):
        if i < len(items):
            go(y_first(i, 0))
            go(y_first(i, 1))

    def y_pump(i):
        for way in range(2):
            y_first(i, way).wait_recv()
            go(y_second(i, way))
        y_start(i + AHEAD)

    def y_wait(i):
        y_second(i, 0).wait_recv()
        y_second(i, 1).wait_recv()

    barrier = pltpu.get_barrier_semaphore()
    for q in range(1, NZ):
        pl.semaphore_signal(barrier, inc=1, device_id=zdev(q), device_id_type=MESH)
    for q in range(1, NT):
        pl.semaphore_signal(barrier, inc=1, device_id=tdev(q), device_id_type=MESH)
    for q in (1, -1):
        pl.semaphore_signal(barrier, inc=1, device_id=ydev(q), device_id_type=MESH)
    my_rows = pl.ds(pl.multiple_of(tp * 16, 16), 16)
    few_copy = pltpu.make_async_copy(hid.at[my_rows, :], hid16, loc_sem.at[10])
    few_copy.start()
    small = []
    for i, (src, dst) in enumerate(((gain_h, gain), (tra_h, tra), (sas_h, sas), (rope_h, rope))):
        copy = pltpu.make_async_copy(src, dst, loc_sem.at[11 + i])
        copy.start()
        small.append(copy)
    hid_copy = pltpu.make_async_copy(hid, hidv, loc_sem.at[0])
    hid_copy.start()

    def inverse_root(ref, rows):
        total = jnp.zeros((16, 128), F32)
        for k in range(8):
            x = ref[rows, pl.ds(k * 1024, 1024)].astype(F32)
            x = x * x
            for m in range(8):
                total = total + x[:, 128 * m : 128 * m + 128]
        return lax.rsqrt(jnp.sum(total, axis=1, keepdims=True) * (1.0 / WIDTH) + 1e-05)

    few_copy.wait()
    for copy in small:
        copy.wait()
    gainf[...] = gain[...].astype(F32)
    s16 = inverse_root(hid16, slice(None))
    for m in range(WIDTH // 128):
        c = slice(128 * m, 128 * m + 128)
        d = 128 * (m % 8)
        asend[m // 8, :, d : d + 128] = (
            hid16[:, c].astype(F32) * s16 * gainf[m : m + 1, :]
        ).astype(BF)

    pl.semaphore_wait(barrier, 7 + 7 + 2)
    for i in range(AHEAD):
        y_start(i)
    own = []
    for i in range(len(items)):
        src, region, _ = items[i]
        copy = pltpu.make_async_copy(src, region(y), loc_sem.at[1 + i])
        copy.start()
        own.append(copy)

    def a_copy(q):
        k = POS[(-q) % NZ]
        return remote(
            asend.at[lax.rem(z + q, NZ)], act.at[k, my_rows, :],
            a_ss.at[k], a_rs.at[k], zdev(q),
        )

    def m_copy(q):
        k = POS[(-q) % NZ]
        return remote(
            meta_s, meta_r.at[:, pl.ds(k * TOK, TOK)], m_ss.at[k], m_rs.at[k], zdev(q)
        )

    for k in FAR_FIRST:
        go(a_copy((-ORDER[k]) % NZ))

    lane = lax.broadcasted_iota(jnp.int32, (TOK, TOK), 1)
    sub = lax.broadcasted_iota(jnp.int32, (TOK, TOK), 0)
    tra_c = jnp.transpose(jnp.broadcast_to(tra[...].astype(F32), (TOK, TOK))).astype(jnp.int32)
    held = sas.shape[1]
    sas_r = jnp.broadcast_to(sas[...].astype(F32), (TOK, held))
    slot_c = jnp.sum(
        jnp.where(tra_c[:, :held] == lane[:, :held], sas_r, 0.0), axis=1, keepdims=True
    )
    slot_cm = jnp.broadcast_to(slot_c, (TOK, TOK))
    slot_rm = jnp.transpose(slot_cm).astype(jnp.int32)
    slot_cm = slot_cm.astype(jnp.int32)
    same = (slot_cm >> 1) == (slot_rm >> 1)
    pos_c = jnp.sum(jnp.where(same & (lane < sub), 1.0, 0.0), axis=1, keepdims=True)
    visb[...] = jnp.where(same & (lane <= sub), 1.0, 0.0)
    flat = (slot_cm >> 3) == (slot_rm >> 3)
    rank_r = jnp.sum(jnp.where(flat & (sub < lane), 1.0, 0.0), axis=0, keepdims=True)
    slot_r = slot_rm[0:1, :]
    code_r = slot_r.astype(F32) * 32.0 + rank_r
    meta_s[...] = jnp.broadcast_to(code_r, (8, TOK))
    meta_r[:, 0:TOK] = jnp.broadcast_to(code_r, (8, TOK))
    for k in FAR_FIRST:
        go(m_copy((-ORDER[k]) % NZ))
    hid_copy.wait()

    def stat(i, carry):
        rows = pl.ds(pl.multiple_of(i * 16, 16), 16)
        scale[rows, :] = jnp.broadcast_to(inverse_root(hidv, rows), (16, 128))
        return carry

    lax.fori_loop(0, 8, stat, 0)

    def normed(b, m):
        c = pl.ds(pl.multiple_of(b * PART + 128 * m, 128), 128)
        g = gainf[pl.ds(pl.multiple_of(b * 8, 8), 8), :]
        return (hidv[:, c].astype(F32) * scale[...] * g[m : m + 1, :]).astype(BF)

    target = (slot_rm >> 3) * ROWS + jnp.broadcast_to(rank_r, (TOK, TOK)).astype(jnp.int32)
    sub2 = lax.broadcasted_iota(jnp.int32, (NZ * ROWS, TOK), 0)
    put = jnp.where(
        sub2 == jnp.concatenate([target, target], axis=0), 1.0, 0.0
    ).astype(BF)
    for m in range(8):
        act[0, :, 128 * m : 128 * m + 128] = normed(tp, m)
    rsend[...] = jnp.dot(put, act[0], preferred_element_type=F32).astype(BF)

    def r_block(b):
        return pl.ds(pl.multiple_of(b * ROWS, ROWS), ROWS)

    def r_copy(q):
        k = POS[(-q) % NZ]
        return remote(
            rsend.at[r_block(lax.rem(z + q, NZ)), :], rrecv.at[pl.ds(k * ROWS, ROWS), :],
            r_ss.at[k], r_rs.at[k], zdev(q),
        )

    for k in FAR_FIRST:
        go(r_copy((-ORDER[k]) % NZ))
    rrecv[0:ROWS, :] = rsend[r_block(z), :]
    for m in range(8):
        act[0, :, 128 * m : 128 * m + 128] = normed(z, m)

    def t_rows(q):
        return pl.ds(pl.multiple_of(lax.rem(tp + q + NT, NT) * 16, 16), 16)

    def x_region(g, q, half=None):
        lo, n = GROUPS[g]
        if half is None:
            return act.at[pl.ds(lo, n), t_rows(q), :]
        return act.at[pl.ds(lo, n), t_rows(q), pl.ds(512 * half, 512)]

    def x_first(g, way):
        ref = x_region(g, 0)
        return remote(ref, ref, x_ss.at[g, way], x_rs.at[g, way], tdev(2 if way == 0 else -2))

    def x_second(g, way):
        ref = x_region(g, -2 if way == 0 else 2, way)
        return remote(
            ref, ref, x_ss.at[g, 2 + way], x_rs.at[g, 2 + way], tdev(2 if way == 0 else -2)
        )

    def p_copy(g, k):
        ref = x_region(g, (0, -2, 2, 4)[k])
        return remote(ref, ref, p_ss.at[g, k], p_rs.at[g, k], partner_dev)

    def x_send(g):
        lo, n = GROUPS[g]
        for k in range(lo, lo + n):
            a_copy((-ORDER[k]) % NZ).wait_recv()
        go(x_first(g, 0))
        go(x_first(g, 1))
        go(p_copy(g, 0))

    def x_forward(g):
        for way in range(2):
            x_first(g, way).wait_recv()
            go(x_second(g, way))
            go(p_copy(g, 1 + way))

    def x_last(g):
        x_second(g, 0).wait_recv()
        x_second(g, 1).wait_recv()
        go(p_copy(g, 3))

    x_send(2)
    y_pump(0)
    x_send(1)
    y_pump(1)
    x_send(0)
    y_pump(2)
    x_forward(2)

    for q in ORDER[1:]:
        m_copy(q).wait_recv()
    a8_row = [jnp.zeros((8, TOK), F32) for _ in range(2)]
    for k in range(NZ):
        code = meta_r[0:8, k * TOK : (k + 1) * TOK]
        code_m = jnp.transpose(jnp.broadcast_to(code[0:1, :], (TOK, TOK))).astype(jnp.int32)
        slot_k = code_m >> 5
        want = jnp.where((slot_k >> 3) == z, (k % 4) * ROWS + (code_m & 31), -1)
        hot = jnp.where(lane == want, 1.0, 0.0).astype(BF)
        place[k] = hot
        a8_of[k] = (slot_k & 7).astype(F32)
        a8 = ((code.astype(jnp.int32) >> 5) & 7).astype(F32).astype(BF)
        a8_row[k // 4] = a8_row[k // 4] + jnp.dot(a8, hot, preferred_element_type=F32)

    x_forward(1)
    y_pump(3)
    x_forward(0)
    y_pump(4)
    x_last(2)
    x_last(1)
    x_last(0)

    low_mine = [None, None]

    def l_copy(g, q):
        return remote(low_s.at[g], low_r.at[g, q], l_ss.at[g, q], l_rs.at[g, q], tdev(q))

    def low_products(g):
        for k in range(max(1, 4 * g), 4 * g + 4):
            r_copy((-ORDER[k]) % NZ).wait_recv()
        low_all = lax.dot_general(
            db[...].reshape(8 * 48, PART), rrecv[TOK * g : TOK * (g + 1), :],
            (((1,), (1,)), ((), ())), preferred_element_type=F32,
        )
        mine = jnp.zeros((48, TOK), F32)
        for a in range(8):
            mine = mine + jnp.where(
                a8_row[g][0:1, :] == float(a), low_all[48 * a : 48 * a + 48, :], 0.0
            )
        low_mine[g] = mine
        low_s[g] = mine.astype(BF)
        for q in range(1, NT):
            go(l_copy(g, q))

    which = ((lax.broadcasted_iota(jnp.int32, (TOK, 384), 1) >> 4) & 7).astype(F32)

    def low_table(g):
        total = low_mine[g]
        for q in range(1, NT):
            l_copy(g, q).wait_recv()
            total = total + low_r[g, q].astype(F32)
        total = total.astype(BF)
        wide = jnp.concatenate(
            [total[0:16]] * 8 + [total[16:32]] * 8 + [total[32:48]] * 8, axis=0
        )
        for k in range(4 * g, 4 * g + 4):
            got = lax.dot_general(
                place[k], wide, (((1,), (1,)), ((), ())), preferred_element_type=F32
            )
            low_l[k] = jnp.where(which == a8_of[k][:, 0:1], got, 0.0).astype(BF)

    def product(c, i):
        a = act[pl.ds(2 * i, 2)].reshape(2 * TOK, PART)
        w = wkvb[...] if c == 0 else wqb[:, CW * (c - 1) : CW * c]
        return jnp.dot(a, w, preferred_element_type=F32).reshape(2, TOK, CW)

    def base(c, g):
        def tile(i, carry):
            part[c, pl.ds(2 * i, 2)] = product(c, i)
            return carry

        lax.fori_loop(2 * g, 2 * g + 2, tile, 0)

    def p_wait(g):
        for k in range(4):
            p_copy(g, k).wait_recv()

    for copy in own:
        copy.wait()
    y_wait(0)
    low_products(1)
    y_pump(5)
    p_wait(2)
    p_wait(1)
    y_wait(1)
    y_wait(2)
    base(0, 1)
    p_wait(0)
    base(0, 0)
    low_products(0)
    low_table(1)
    y_wait(3)
    y_wait(4)

    def z_copy(c, way, h):
        k = POS[h if way == 0 else NZ - h]
        return remote(
            sendb.at[c, k], recvb.at[c, way, h - 1], z_ss.at[c, way, h - 1],
            z_rs.at[c, way, h - 1], zdev(1 if way == 0 else -1),
        )

    def change(c, i):
        ll = low_l[pl.ds(2 * i, 2)].reshape(2 * TOK, 384)
        if c == 0:
            u_k = ukvb[:, 0:16, :].reshape(128, 128)
            u_v = ukvb[:, 16:32, :].reshape(128, 128)
            d = jnp.concatenate(
                [
                    jnp.dot(ll[:, 128:256], u_k, preferred_element_type=F32),
                    jnp.dot(ll[:, 256:384], u_v, preferred_element_type=F32),
                ],
                axis=1,
            )
        else:
            u_q = uqb[:, :, CW * (c - 1) : CW * c].reshape(128, CW)
            d = jnp.dot(ll[:, 0:128], u_q, preferred_element_type=F32)
        return (0.5 * d.astype(BF).astype(F32)).reshape(2, TOK, CW)

    def complete(c, g):
        def tile(i, carry):
            here = product(c, i) if c > 0 else part[c, pl.ds(2 * i, 2)]
            part[c, pl.ds(2 * i, 2)] = here + change(c, i)
            return carry

        lax.fori_loop(2 * g, 2 * g + 2, tile, 0)

    def ring(c, h):
        for way in range(2):
            if h > longest(c, way):
                continue
            k = POS[h if way == 0 else NZ - h]
            total = part[c, k]
            if h + 1 <= longest(c, way):
                z_copy(c, way, h + 1).wait_recv()
                total = total + recvb[c, way, h].astype(F32)
            sendb[c, k] = total.astype(BF)
            go(z_copy(c, way, h))

    complete(0, 1)
    ring(0, 4)
    y_pump(6)
    low_table(0)
    y_pump(7)
    y_wait(5)
    complete(1, 1)
    ring(1, 4)
    complete(0, 0)
    ring(0, 3)
    y_pump(8)
    complete(1, 0)
    ring(1, 3)
    for c in range(2, CHUNKS):
        y_wait(4 + c)
        complete(c, 1)
        ring(c, 4)
    for c in range(2, CHUNKS):
        ring(c, 3)
        complete(c, 0)
    for c in range(CHUNKS):
        ring(c, 2)
    pos_m = jnp.broadcast_to(pos_c, (TOK, TOK))
    cos = jnp.zeros((TOK, TOK), F32)
    sin = jnp.zeros((TOK, TOK), F32)
    for p in range(8):
        here = pos_m == float(p)
        cos = jnp.where(here, rope[p : p + 1, :], cos)
        sin = jnp.where(here, rope[8 + p : 9 + p, :], sin)
    cosb[...] = cos
    sinb[...] = sin

    for c in range(CHUNKS):
        ring(c, 1)

    def final(c):
        z_copy(c, 0, 1).wait_recv()
        z_copy(c, 1, 1).wait_recv()
        return part[c, 0] + recvb[c, 0, 0].astype(F32) + recvb[c, 1, 0].astype(F32)

    cos = cosb[...]
    sin = sinb[...]

    def turn(u):
        return u * cos + pltpu.roll(u, HEAD // 2, 1) * sin

    kv = final(0)
    keys = turn(kv[:, 0:HEAD]).astype(BF)
    values = kv[:, HEAD:].astype(BF)
    kout[...] = keys
    vout[...] = values
    seen = visb[...] > 0.5
    root = float(np.float32(1.0) / np.sqrt(np.float32(HEAD)))
    for c in range(1, CHUNKS):
        both = final(c)
        for i in range(2):
            query = turn(both[:, HEAD * i : HEAD * (i + 1)]).astype(BF)
            scores = lax.dot_general(
                query, keys, (((1,), (1,)), ((), ())), preferred_element_type=F32
            ) * root
            scores = jnp.where(seen, scores, -1e30)
            raised = jnp.exp(scores - jnp.max(scores, axis=1, keepdims=True))
            weights = (raised / jnp.sum(raised, axis=1, keepdims=True)).astype(BF)
            lo = CW * (c - 1) + HEAD * i
            ctx[:, lo : lo + HEAD] = jnp.dot(
                weights, values, preferred_element_type=F32
            ).astype(BF)

    for copy in pending:
        copy.wait_send()


def forward(a, b, c, ao, bo, co):
    ao[...] = a[...]
    bo[...] = b[...]
    co[...] = c[...]


def rope_table():
    half = HEAD // 2
    freq = np.float32(10000.0) ** (-(np.arange(half, dtype=np.float32) * np.float32(2.0) / HEAD))
    angle = np.arange(8, dtype=np.float32)[:, None] * freq[None, :].astype(np.float32)
    cos = np.cos(angle).astype(np.float32)
    sin = np.sin(angle).astype(np.float32)
    return np.concatenate(
        [np.concatenate([cos, cos], axis=1), np.concatenate([-sin, sin], axis=1)], axis=0
    )


def per_device(hidden, gain, wq, wk, wv, down, up_q, up_kv, adapter, storage):
    any_spec = pl.BlockSpec(memory_space=pl.ANY)
    vmem = pl.BlockSpec(memory_space=pltpu.VMEM)
    dma = pltpu.SemaphoreType.DMA
    count = storage.shape[0]
    call = pl.pallas_call(
        body,
        out_shape=(
            jax.ShapeDtypeStruct((TOK, PART), BF),
            jax.ShapeDtypeStruct((TOK, HEAD), BF),
            jax.ShapeDtypeStruct((TOK, HEAD), BF),
        ),
        in_specs=[any_spec] * 11,
        out_specs=(vmem, vmem, vmem),
        scratch_shapes=[
            pltpu.VMEM((WIDTH // 128, 128), BF),
            pltpu.VMEM((1, TOK), jnp.int32),
            pltpu.VMEM((1, count), jnp.int32),
            pltpu.VMEM((16, 128), F32),
            pltpu.VMEM((TOK, WIDTH), BF),
            pltpu.VMEM((16, WIDTH), BF),
            pltpu.VMEM((WIDTH // 128, 128), F32),
            pltpu.VMEM((TOK, 128), F32),
            pltpu.VMEM((NZ, TOK, PART), BF),
            pltpu.VMEM((NZ, 16, PART), BF),
            pltpu.VMEM((8, TOK), F32),
            pltpu.VMEM((8, NZ * TOK), F32),
            pltpu.VMEM((NZ * ROWS, PART), BF),
            pltpu.VMEM((NZ * ROWS, PART), BF),
            pltpu.VMEM((PART, PART), BF),
            pltpu.VMEM((PART, CW), BF),
            pltpu.VMEM((8, 48, PART), BF),
            pltpu.VMEM((8, 16, PART), BF),
            pltpu.VMEM((8, 32, HEAD), BF),
            pltpu.VMEM((NZ, TOK, TOK), BF),
            pltpu.VMEM((NZ, TOK, 128), F32),
            pltpu.VMEM((2, 48, TOK), BF),
            pltpu.VMEM((2, NT, 48, TOK), BF),
            pltpu.VMEM((NZ, TOK, 384), BF),
            pltpu.VMEM((CHUNKS, NZ, TOK, CW), F32),
            pltpu.VMEM((CHUNKS, NZ, TOK, CW), BF),
            pltpu.VMEM((CHUNKS, 2, 4, TOK, CW), BF),
            pltpu.VMEM((TOK, TOK), F32),
            pltpu.VMEM((TOK, TOK), F32),
            pltpu.VMEM((TOK, TOK), F32),
            dma((15,)),
            dma((9, 4)), dma((9, 4)),
            dma((NZ,)), dma((NZ,)),
            dma((NZ,)), dma((NZ,)),
            dma((NZ,)), dma((NZ,)),
            dma((3, 4)), dma((3, 4)),
            dma((3, 4)), dma((3, 4)),
            dma((2, NT)), dma((2, NT)),
            dma((CHUNKS, 2, 4)), dma((CHUNKS, 2, 4)),
        ],
        compiler_params=pltpu.CompilerParams(
            collective_id=0, has_side_effects=True, vmem_limit_bytes=60 * 1024 * 1024
        ),
    )
    outs = call(
        hidden,
        gain.reshape(WIDTH // 128, 128),
        adapter.reshape(1, TOK),
        storage.reshape(1, count),
        jnp.asarray(rope_table()),
        wq, wk, wv, down, up_q, up_kv,
    )
    return pl.pallas_call(
        forward,
        out_shape=tuple(jax.ShapeDtypeStruct(o.shape, o.dtype) for o in outs),
        in_specs=[vmem] * 3,
        out_specs=(vmem,) * 3,
    )(*outs)


def solution(mesh):
    in_specs = (
        P("req", None),
        P(),
        P("req", "tp"),
        P("req", "tp"),
        P("req", "tp"),
        P("req", None, "tp"),
        P("req", None, "tp"),
        P("req", None, "tp"),
        P("req"),
        P(),
    )
    out_specs = (P("req", "tp"), P("req", "tp"), P("req", "tp"))
    return jax.shard_map(
        per_device, mesh=mesh, in_specs=in_specs, out_specs=out_specs, check_vma=False
    )
```
